32 devices in a mesh: row: 4 (over y, x), col: 8 (over z, core).
Axes of the slice: x: 2, y: 2, z: 4, core: 2. Of those that a mesh axis runs over, the one named last changes fastest.
Arguments:
- rhs: float32 [1536, 3072], P('row', 'col'), may hold values from -6 to 6
- a_coupling: bfloat16 [3, 1536, 3072], P(None, 'row', 'col'), may hold values from -0.3125 to 0.3125
- b_coupling: bfloat16 [3, 1536, 3072], P(None, 'row', 'col'), may hold values from -0.3125 to 0.3125
- a_basis: float32 [1536, 384], P('row'), may hold values from -0.3125 to 0.3125
- b_basis: float32 [3072, 384], P('col'), may hold values from -0.3125 to 0.3125
- a_vals: float32 [1536], P('row'), may hold values from 0.25 to 4
- b_vals: float32 [3072], P('col'), may hold values from 0.25 to 4
Outputs:
- solution: bfloat16 [1536, 3072], P('row', 'col')
- rhs_next: float32 [1536, 3072], P('row', 'col')
The draws below stay inside these ranges and needn't reach their ends.
All inputs are finite; a program needn't handle non-finite values.
Results may differ from the reference program's by a relative error of at most 0.0037.
Values may be sent and summed in bfloat16 or wider, within the bound.
No kernel may reach another device: no remote copies, remote signals or barrier semaphores. Data moves between devices by JAX's collectives and lax.ppermute only.
A program may use at most 64 MiB of HBM per device.

```python
import math
import jax
import jax.numpy as jnp
from jax import lax

BS = 384
ROWS_X = 1536
COLS_X = 3072
START = 4
N_ROW = 4
N_COL = 8


def levels(rng, shape, pieces, least, high):
    loudness, own = 1.0, jax.random.fold_in(rng, 6)
    for dim, shards_of in pieces:
        draws = jnp.exp(jax.random.uniform(jax.random.fold_in(own, dim), (shards_of,), jnp.float32, least / len(pieces), high / len(pieces)))
        loudness = loudness * jnp.repeat(draws, shape[dim] // shards_of).reshape([-1 if axis == dim else 1 for axis in range(len(shape))])
    return loudness


def normal_values(stream_key, extent, scale, bound, pieces=(), kind=jnp.bfloat16):
    gain = levels(stream_key, extent, pieces, -0.22, 0.18) if pieces else 1.0
    array = jax.random.normal(stream_key, extent, jnp.float32) * scale * gain
    return jnp.minimum(jnp.maximum(array, -bound), bound).astype(kind)


def setup_inputs(seed: int = 0) -> dict:
    keys = jax.random.split(jax.random.key(seed), 8)
    rhs = normal_values(keys[0], (ROWS_X, COLS_X), 1.0, 6.0, ((0, 4), (1, 8)), jnp.float32)
    a_coupling = normal_values(keys[1], (3, ROWS_X, COLS_X), BS ** -0.5, 0.3125, ((1, 4), (2, 8)))
    b_coupling = normal_values(keys[2], (3, ROWS_X, COLS_X), BS ** -0.5, 0.3125, ((1, 4), (2, 8)))
    a_basis = normal_values(keys[3], (ROWS_X, BS), BS ** -0.5, 0.3125, ((0, 4),), jnp.float32)
    b_basis = normal_values(keys[4], (COLS_X, BS), BS ** -0.5, 0.3125, ((0, 8),), jnp.float32)
    a_vals = jnp.clip(jnp.exp(math.log(4.0) - 2.7725887 * jax.random.uniform(keys[5], (ROWS_X,), jnp.float32) ** levels(keys[5], (ROWS_X,), ((0, 4),), -0.2, 0.2)), 0.25, 4.0)
    b_vals = jnp.clip(jnp.exp(math.log(4.0) - 2.7725887 * jax.random.uniform(keys[6], (COLS_X,), jnp.float32) ** levels(keys[6], (COLS_X,), ((0, 8),), -0.2, 0.2)), 0.25, 4.0)
    return dict(rhs=rhs, a_coupling=a_coupling, b_coupling=b_coupling, a_basis=a_basis, b_basis=b_basis, a_vals=a_vals, b_vals=b_vals)


def reference(rhs, a_coupling, b_coupling, a_basis, b_basis, a_vals, b_vals):
    highest = lax.Precision.HIGHEST
    rows_n = N_ROW
    cols_n = N_COL
    state = rhs.reshape(rows_n, BS, cols_n, BS).transpose(0, 2, 1, 3)
    basis_a = a_basis.reshape(rows_n, BS, BS)
    basis_b = b_basis.reshape(cols_n, BS, BS)
    vals_a = a_vals.reshape(rows_n, BS)
    vals_b = b_vals.reshape(cols_n, BS)
    row_ids = jnp.arange(rows_n, dtype=jnp.int32)
    row_grid = jnp.broadcast_to(row_ids[:, None], (rows_n, cols_n))
    col_grid = jnp.broadcast_to(jnp.arange(cols_n, dtype=jnp.int32)[None, :], (rows_n, cols_n))
    level = rows_n - 1 - row_grid + col_grid
    solution = jnp.zeros((rows_n, cols_n, BS, BS), jnp.bfloat16)
    for step in range(3):
        col_of = row_ids - rows_n + 1 + START + step
        col_valid = (col_of >= 0) & (col_of < cols_n)
        col_safe = jnp.clip(col_of, 0, cols_n - 1).astype(jnp.int32)
        picked = state[row_ids, col_safe]
        left_basis = basis_a
        right_basis = basis_b[col_safe]
        inner = jnp.einsum('iap,iab->ipb', left_basis, picked, precision=highest)
        inner = jnp.einsum('ipb,ibq->ipq', inner, right_basis, precision=highest)
        inner = inner / (vals_a[:, :, None] + vals_b[col_safe][:, None, :])
        outer = jnp.einsum('iap,ipq->iaq', left_basis, inner, precision=highest)
        outer = jnp.einsum('iaq,ibq->iab', outer, right_basis, precision=highest)
        outer = jnp.where(col_valid[:, None, None], outer, 0.0).astype(jnp.bfloat16)
        fresh = jnp.zeros((rows_n, cols_n, BS, BS), jnp.bfloat16).at[row_ids, col_safe].set(outer)
        solution = solution + fresh
        k_index = col_grid + rows_n - 1 - START - step
        k_valid = (k_index > row_grid) & (k_index < rows_n)
        down = fresh[jnp.clip(k_index, 0, rows_n - 1).astype(jnp.int32), col_grid]
        m_index = row_grid + START + step - rows_n + 1
        m_valid = (m_index >= 0) & (m_index < col_grid)
        left = fresh[row_grid, jnp.clip(m_index, 0, cols_n - 1).astype(jnp.int32)]
        coup_a = a_coupling[step].reshape(rows_n, BS, cols_n, BS).transpose(0, 2, 1, 3)
        coup_b = b_coupling[step].reshape(rows_n, BS, cols_n, BS).transpose(0, 2, 1, 3)
        term_down = jnp.einsum('ijab,ijbc->ijac', coup_a.astype(jnp.float32), down.astype(jnp.float32), precision=highest)
        term_left = jnp.einsum('ijab,ijbc->ijac', left.astype(jnp.float32), coup_b.astype(jnp.float32), precision=highest)
        term_down = jnp.where(k_valid[:, :, None, None], term_down, 0.0)
        term_left = jnp.where(m_valid[:, :, None, None], term_left, 0.0)
        state = state - (term_down + term_left)
    later = (level > START + 2)[:, :, None, None]
    rhs_next = jnp.where(later, state, 0.0)
    solution = solution.transpose(0, 2, 1, 3).reshape(rows_n * BS, cols_n * BS)
    rhs_next = rhs_next.transpose(0, 2, 1, 3).reshape(rows_n * BS, cols_n * BS)
    return solution, rhs_next
```

```python
import functools

import jax
import jax.numpy as jnp
from jax import lax
from jax.experimental import pallas as pl
from jax.experimental.pallas import tpu as pltpu
from jax.sharding import PartitionSpec as P

AXES = ("row", "col")
VMEM_SPEC = pl.BlockSpec(memory_space=pltpu.VMEM)
ANY_SPEC = pl.BlockSpec(memory_space=pl.ANY)


def plan(rows_n, cols_n, offset, gap, up_gap):
    todo = []
    for i in range(rows_n):
        m = i + offset
        if 0 <= m < cols_n:
            targets = range(m + gap, cols_n)
            chips = sorted({j // 2 for j in targets}, reverse=True)
            for chip in chips:
                todo.append(("left", (i, m), [(i, j) for j in targets if j // 2 == chip]))
            if i - up_gap >= 0:
                todo.append(("down", (i, m), [(k, m) for k in range(i - up_gap, -1, -1)]))
    ops, forwards = [], []
    while todo or forwards:
        used_from, used_to, op, later = set(), set(), [], []

        def take(source, target, kind, forward):
            if source in used_from or target in used_to:
                return False
            used_from.add(source)
            used_to.add(target)
            op.append((source, target, kind, forward))
            return True

        kept = []
        for item in forwards:
            ready, source, target = item
            if not (ready <= len(ops) and take(source, target, "left", ready - 2)):
                kept.append(item)
        forwards = kept
        order = sorted(todo, key=lambda item: (item[0] == "down", len(item[2]) == 1))
        for item in order:
            kind, source, targets = item
            if kind == "left":
                for target in targets:
                    if take(source, target, kind, None):
                        todo.remove(item)
                        rest = [other for other in targets if other != target]
                        later += [(len(ops) + 2, target, other) for other in rest]
                        break
            else:
                for target in targets:
                    if take(source, target, kind, None):
                        targets.remove(target)
                        break
                if not targets:
                    todo.remove(item)
        forwards += later
        ops.append(op)
    return ops


def one_of(me, ids):
    hit = me < 0
    for each in sorted(ids):
        hit = hit | (me == each)
    return hit


def place(cols_n):
    return lax.axis_index("row") * cols_n + lax.axis_index("col")


def level_of(rows_n):
    return rows_n - 1 - lax.axis_index("row") + lax.axis_index("col")


def dot(a, b):
    return lax.dot_general(a, b, (((1,), (0,)), ((), ())), preferred_element_type=jnp.float32)


def split(x):
    high = x.astype(jnp.bfloat16)
    return high, (x - high.astype(jnp.float32)).astype(jnp.bfloat16)


def put_left(ref, pair):
    n = pair[0].shape[1]
    ref[:, 0:n] = pair[0]
    ref[:, n : 2 * n] = pair[0]
    ref[:, 2 * n : 3 * n] = pair[1]


def put_right(ref, pair):
    n = pair[0].shape[0]
    ref[0:n] = pair[0]
    ref[n : 2 * n] = pair[1]
    ref[2 * n : 3 * n] = pair[0]


def solve(state, uk, utk, vk, vtk, inverse, lhs, rhs):
    put_left(lhs, split(state))
    part = dot(lhs[...], vk[...])
    put_right(rhs, split(part))
    part = dot(utk[...], rhs[...]) * inverse[...]
    put_left(lhs, split(part))
    part = dot(lhs[...], vtk[...])
    put_right(rhs, split(part))
    return dot(uk[...], rhs[...]).astype(jnp.bfloat16)


def copies(pairs, sem):
    moves = [pltpu.make_async_copy(source, target, sem.at[n]) for n, (source, target) in enumerate(pairs)]
    for move in moves:
        move.start()
    return moves


def begin(rows_n, first, rhs, a_c, b_c, u_any, v_any, av, bv, f0, uk, utk, vk, vtk, inverse, s, ca, cb, u, v, lhs, mid, sem):
    level = level_of(rows_n)

    @pl.when((level >= first) & (level <= first + 2))
    def _():
        moves = copies(((u_any, u), (v_any, v), (rhs, s), (a_c.at[0], ca), (b_c.at[0], cb)), sem)
        n = u.shape[0]
        alpha = jnp.transpose(jnp.broadcast_to(av[...], (128, n)))
        for c in range(0, n, 128):
            inverse[:, c : c + 128] = 1.0 / (alpha + bv[:, c : c + 128])
        moves[0].wait()
        high, low = split(u[...])
        put_left(uk, (high, low))
        put_left(utk, (high.T, low.T))
        moves[1].wait()
        high, low = split(v[...])
        put_right(vk, (high, low))
        put_right(vtk, (high.T, low.T))
        moves[2].wait()
        moves[3].wait()
        moves[4].wait()

    @pl.when(level == first)
    def _():
        f0[...] = solve(s[...], uk, utk, vk, vtk, inverse, lhs, mid)


def second(rows_n, first, down, left, uk, utk, vk, vtk, inverse, s, ca, cb, f1, pair_l, pair_d, lhs, mid):
    @pl.when(level_of(rows_n) == first + 1)
    def _():
        n = s.shape[0]
        state = s[...] - (dot(ca[...], down[...]) + dot(left[...], cb[...]))
        block = solve(state, uk, utk, vk, vtk, inverse, lhs, mid)
        f1[...] = block
        pair_l[0:n] = left[...]
        pair_l[n:] = block
        pair_d[0:n] = down[...]
        pair_d[n:] = block


def third_early(rows_n, first, a_c, b_c, down, left, s, ca, cb, s1, a1, b1, sem):
    @pl.when(level_of(rows_n) == first + 2)
    def _():
        moves = copies(((a_c.at[1], a1), (b_c.at[1], b1)), sem)
        s1[...] = s[...] - (dot(ca[...], down[...]) + dot(left[...], cb[...]))
        for move in moves:
            move.wait()


def third(rows_n, cols_n, first, ops, rhs, a_c, b_c, down, left, uk, utk, vk, vtk, inverse, s1, a1, b1, *rest):
    arrived, (f2, s2, a2, b2, lhs, mid, av, bv, got, sem) = rest[: len(ops)], rest[len(ops) :]
    level = level_of(rows_n)

    @pl.when(level == first + 2)
    def _():
        state = s1[...] - (dot(a1[...], down[...]) + dot(left[...], b1[...]))
        f2[...] = solve(state, uk, utk, vk, vtk, inverse, lhs, mid)

    @pl.when(level > first + 2)
    def _():
        n = s2.shape[0]
        moves = copies(((rhs, s2), (a_c.at[0:2], av), (b_c.at[0:2], bv), (a_c.at[2], a2), (b_c.at[2], b2)), sem)
        for move in moves:
            move.wait()
        for kind in ("left", "down"):
            hits = pick(cols_n, ops, kind, arrived, got)

            @pl.when(hits)
            def _():
                for t in range(2):
                    block = got[t * n : (t + 1) * n]
                    s2[...] -= dot(block, bv[t]) if kind == "left" else dot(av[t], block)


def pick(cols_n, ops, kind, arrived, got):
    me = place(cols_n)
    any_hit = me < 0
    for op, ref in zip(ops, arrived):
        hit = one_of(me, [t[0] * cols_n + t[1] for _, t, k, _ in op if k == kind])
        any_hit = any_hit | hit

        @pl.when(hit)
        def _():
            got[...] = ref[...]

    return any_hit


def finish(rows_n, cols_n, first, ops, f0, f1, f2, s2, a2, b2, *rest):
    arrived, (out, nxt, got) = rest[: len(ops)], rest[len(ops) :]
    level = level_of(rows_n)
    out[...] = jnp.zeros(out.shape, out.dtype)
    for t, block in enumerate((f0, f1, f2)):

        @pl.when(level == first + t)
        def _():
            out[...] = block[...]

    @pl.when(level <= first + 2)
    def _():
        nxt[...] = jnp.zeros(nxt.shape, nxt.dtype)

    @pl.when(level > first + 2)
    def _():
        nxt[...] = s2[...]
        for kind in ("down", "left"):
            hits = pick(cols_n, ops, kind, arrived, got)

            @pl.when(hits)
            def _():
                nxt[...] -= dot(got[...], b2[...]) if kind == "left" else dot(a2[...], got[...])


def spread(ops, cols_n, own):
    me = place(cols_n)
    arrived = []
    for op in ops:
        value = own["left"]
        if own["down"] is not own["left"]:
            downs = [s[0] * cols_n + s[1] for s, _, k, _ in op if k == "down"]
            if downs:
                value = jnp.where(one_of(me, downs), own["down"], value)
        for earlier in sorted({f for *_, f in op if f is not None}):
            ids = [s[0] * cols_n + s[1] for s, _, _, f in op if f == earlier]
            value = jnp.where(one_of(me, ids), arrived[earlier], value)
        pairs = [(s[0] * cols_n + s[1], t[0] * cols_n + t[1]) for s, t, _, _ in op]
        arrived.append(lax.ppermute(value, AXES, pairs))
    return arrived


def solution(mesh):
    rows_n, cols_n = mesh.shape["row"], mesh.shape["col"]
    first = (rows_n + cols_n) // 2 - 2
    offset = first - rows_n + 1
    pair_ops = plan(rows_n, cols_n, offset + 1, 2, 2)
    last_ops = plan(rows_n, cols_n, offset + 2, 1, 1)

    def owners(t):
        return [(i, i + offset + t) for i in range(rows_n) if 0 <= i + offset + t < cols_n]

    def up(t, far):
        return [(i * cols_n + j, (i - far) * cols_n + j) for i, j in owners(t) if i >= far]

    def right(t, far):
        return [(i * cols_n + j, i * cols_n + j + far) for i, j in owners(t) if j + far < cols_n]

    def shards(rhs, a_c, b_c, u, v, a_vals, b_vals):
        n = rhs.shape[0]
        half, full = jnp.bfloat16, jnp.float32
        square = jax.ShapeDtypeStruct((n, n), half)
        wide, tall = jax.ShapeDtypeStruct((n, 3 * n), half), jax.ShapeDtypeStruct((3 * n, n), half)
        pair = jax.ShapeDtypeStruct((2 * n, n), half)
        state = jax.ShapeDtypeStruct((n, n), full)
        work = [pltpu.VMEM((n, 3 * n), half), pltpu.VMEM((3 * n, n), half)]

        def call(kernel, ins, outs, scratch, name):
            return pl.pallas_call(
                kernel,
                out_shape=outs,
                in_specs=[ANY_SPEC if far else VMEM_SPEC for _, far in ins],
                out_specs=[VMEM_SPEC] * len(outs),
                scratch_shapes=scratch,
                compiler_params=pltpu.CompilerParams(vmem_limit_bytes=24 << 20),
                name=name,
            )(*[x for x, _ in ins])

        def hbm(*xs):
            return [(x, True) for x in xs]

        def near(*xs):
            return [(x, False) for x in xs]

        f0, uk, utk, vk, vtk, inverse, s, ca, cb = call(
            functools.partial(begin, rows_n, first),
            hbm(rhs, a_c, b_c, u, v) + near(a_vals.reshape(1, n), b_vals.reshape(1, n)),
            [square, wide, wide, tall, tall, state, state, square, square],
            [pltpu.VMEM((n, n), full)] * 2 + work + [pltpu.SemaphoreType.DMA((5,))],
            "begin",
        )
        basis = near(uk, utk, vk, vtk, inverse)
        down = lax.ppermute(f0, AXES, up(0, 1))
        left = lax.ppermute(f0, AXES, right(0, 1))
        down_far = lax.ppermute(f0, AXES, up(0, 2))
        left_far = lax.ppermute(f0, AXES, right(0, 2))
        f1, pair_l, pair_d = call(
            functools.partial(second, rows_n, first),
            near(down, left) + basis + near(s, ca, cb),
            [square, pair, pair],
            work,
            "second",
        )
        down = lax.ppermute(f1, AXES, up(1, 1))
        left = lax.ppermute(f1, AXES, right(1, 1))
        s1, a1, b1 = call(
            functools.partial(third_early, rows_n, first),
            hbm(a_c, b_c) + near(down_far, left_far, s, ca, cb),
            [state, square, square],
            [pltpu.SemaphoreType.DMA((2,))],
            "third_early",
        )
        pairs = spread(pair_ops, cols_n, {"left": pair_l, "down": pair_d})
        f2, s2, a2, b2 = call(
            functools.partial(third, rows_n, cols_n, first, pair_ops),
            hbm(rhs, a_c, b_c) + near(down, left) + basis + near(s1, a1, b1, *pairs),
            [square, state, square, square],
            work
            + [pltpu.VMEM((2, n, n), half)] * 2
            + [pltpu.VMEM((2 * n, n), half), pltpu.SemaphoreType.DMA((5,))],
            "third",
        )
        lasts = spread(last_ops, cols_n, {"left": f2, "down": f2})
        return call(
            functools.partial(finish, rows_n, cols_n, first, last_ops),
            near(f0, f1, f2, s2, a2, b2, *lasts),
            [square, state],
            [pltpu.VMEM((n, n), half)],
            "finish",
        )

    placed = (
        P("row", "col"),
        P(None, "row", "col"),
        P(None, "row", "col"),
        P("row", None),
        P("col", None),
        P("row"),
        P("col"),
    )
    return jax.shard_map(
        shards,
        mesh=mesh,
        in_specs=placed,
        out_specs=(P("row", "col"), P("row", "col")),
        check_vma=False,
    )
```

```python
import functools

import jax
import jax.numpy as jnp
from jax import lax
from jax.experimental import pallas as pl
from jax.experimental.pallas import tpu as pltpu
from jax.sharding import PartitionSpec as P


AXES = ("row", "col")
VMEM_SPEC = pl.BlockSpec(memory_space=pltpu.VMEM)
FAR_SPEC = pl.BlockSpec(memory_space=pltpu.HBM)


def plan(rows_n, cols_n, offset, gap, up_gap):
    rights, ups = [], []
    for i in range(rows_n):
        m = i + offset
        if 0 <= m < cols_n:
            targets = range(m + gap, cols_n)
            for chip in sorted({j // 2 for j in targets}, reverse=True):
                rights.append(((i, m), [(i, j) for j in targets if j // 2 == chip]))
            ups += [((i, m), (k, m)) for k in range(i - up_gap, -1, -1)]
    ops, forwards = [], []
    while rights or ups:
        used_from, used_to, op = set(), set(), []

        def take(source, target, kind):
            if source in used_from or target in used_to:
                return False
            used_from.add(source)
            used_to.add(target)
            op.append((source, target, kind, None))
            return True

        for item in list(rights):
            source, targets = item
            waiting = [t for _, t in ups]
            for target in sorted(targets, key=lambda t: t in waiting):
                if take(source, target, "left"):
                    rights.remove(item)
                    forwards += [(target, other, "left", len(ops)) for other in targets if other != target]
                    break
        for item in list(ups):
            if take(*item, "down"):
                ups.remove(item)
        ops.append(op)
    return ops + [forwards] if forwards else ops


def one_of(me, ids):
    hit = me < 0
    for each in sorted(ids):
        hit = hit | (me == each)
    return hit


def place(cols_n):
    return lax.axis_index("row") * cols_n + lax.axis_index("col")


def level_of(rows_n):
    return rows_n - 1 - lax.axis_index("row") + lax.axis_index("col")


def dot(a, b):
    return lax.dot_general(a, b, (((1,), (0,)), ((), ())), preferred_element_type=jnp.float32)


def split(x):
    high = x.astype(jnp.bfloat16)
    return high, (x - high.astype(jnp.float32)).astype(jnp.bfloat16)


def put_left(ref, pair):
    n = pair[0].shape[1]
    ref[:, 0:n] = pair[0]
    ref[:, n : 2 * n] = pair[0]
    ref[:, 2 * n : 3 * n] = pair[1]


def put_right(ref, pair):
    n = pair[0].shape[0]
    ref[0:n] = pair[0]
    ref[n : 2 * n] = pair[1]
    ref[2 * n : 3 * n] = pair[0]


def dot_t(a, b):
    return lax.dot_general(a, b, (((1,), (1,)), ((), ())), preferred_element_type=jnp.float32)


def solve(state, uk, utk, vk, vl, inverse, lhs, mid):
    put_left(lhs, split(state))
    part = dot(lhs[...], vk[...])
    put_right(mid, split(part))
    part = dot(utk[...], mid[...]) * inverse[...]
    put_left(lhs, split(part))
    part = dot_t(lhs[...], vl[...])
    put_right(mid, split(part))
    return dot(uk[...], mid[...]).astype(jnp.bfloat16)


def put_lanes(ref, pair):
    n = pair[0].shape[1]
    ref[:, 0:n] = pair[0]
    ref[:, n : 2 * n] = pair[1]
    ref[:, 2 * n : 3 * n] = pair[0]


def set_inverse(inverse, av, bv):
    n = inverse.shape[0]
    alpha = jnp.transpose(jnp.broadcast_to(av[...][None, :], (128, n)))
    beta = bv[...][None, :]
    for c in range(0, n, 128):
        inverse[:, c : c + 128] = 1.0 / (alpha + beta[:, c : c + 128])


def set_right_basis(v, vk, vl):
    pair = split(v[...])
    put_right(vk, pair)
    put_lanes(vl, pair)


def set_left_basis(u, uk, utk):
    high, low = split(u[...])
    put_left(uk, (high, low))
    put_left(utk, (high.T, low.T))


def copies(pairs, sem):
    moves = [pltpu.make_async_copy(source, target, sem.at[n]) for n, (source, target) in enumerate(pairs)]
    for move in moves:
        move.start()
    return moves


def begin(rows_n, first, rhs, u_far, v_far, a_vals, b_vals, f0, s, u, v, av, bv, uk, utk, vk, vl, inverse, lhs, mid, sem):
    @pl.when(level_of(rows_n) == first)
    def _():
        moves = copies(((v_far, v), (rhs, s), (u_far, u), (a_vals, av), (b_vals, bv)), sem)
        moves[0].wait()
        set_right_basis(v, vk, vl)
        for move in moves[1:]:
            move.wait()
        set_left_basis(u, uk, utk)
        set_inverse(inverse, av, bv)
        f0[...] = solve(s[...], uk, utk, vk, vl, inverse, lhs, mid)


def prepare(rows_n, first, rhs, a_c, b_c, u_far, v_far, a_vals, b_vals, uk, utk, vk, vl, inverse, s, ca, cb, u, v, av, bv, sem):
    level = level_of(rows_n)

    @pl.when((level > first) & (level <= first + 2))
    def _():
        moves = copies(((v_far, v), (u_far, u), (a_vals, av), (b_vals, bv), (rhs, s), (a_c.at[0], ca), (b_c.at[0], cb)), sem)
        moves[0].wait()
        set_right_basis(v, vk, vl)
        moves[1].wait()
        set_left_basis(u, uk, utk)
        moves[2].wait()
        moves[3].wait()
        set_inverse(inverse, av, bv)
        for move in moves[4:]:
            move.wait()


def second(rows_n, first, down, left, uk, utk, vk, vl, inverse, s, ca, cb, f1, lhs, mid):
    @pl.when(level_of(rows_n) == first + 1)
    def _():
        state = s[...] - (dot(ca[...], down[...]) + dot(left[...], cb[...]))
        f1[...] = solve(state, uk, utk, vk, vl, inverse, lhs, mid)


def third_early(rows_n, first, rhs, a_c, b_c, down, direct, on_chip, s1, a1, b1, a0, b0, sem):
    even = lax.rem(lax.axis_index("col"), 2) == 0

    @pl.when(level_of(rows_n) == first + 2)
    def _():
        moves = copies(((rhs, s1), (a_c.at[0], a0), (b_c.at[0], b0), (a_c.at[1], a1), (b_c.at[1], b1)), sem)
        for move in moves:
            move.wait()
        left = jnp.where(even, direct[...], on_chip[...])
        s1[...] -= dot(a0[...], down[...]) + dot(left, b0[...])


def third(rows_n, first, down, left, uk, utk, vk, vl, inverse, s1, a1, b1, f2, lhs, mid):
    @pl.when(level_of(rows_n) == first + 2)
    def _():
        state = s1[...] - (dot(a1[...], down[...]) + dot(left[...], b1[...]))
        f2[...] = solve(state, uk, utk, vk, vl, inverse, lhs, mid)


def subtract(cols_n, ops, arrived, got, state, coup_a, coup_b, out, kinds=("down", "left")):
    out[...] = state[...]
    for kind in kinds:
        hits = pick(cols_n, ops, kind, arrived, got)

        @pl.when(hits)
        def _():
            out[...] -= dot(got[...], coup_b[...]) if kind == "left" else dot(coup_a[...], got[...])


def middle(rows_n, cols_n, first, ops, rhs, a_c, b_c, *rest):
    arrived, (s1, a1, b1, a2, b2, s, a0, b0, got, sem) = rest[: len(ops)], rest[len(ops) :]

    @pl.when(level_of(rows_n) > first + 2)
    def _():
        pairs = ((rhs, s), (a_c.at[0], a0), (b_c.at[0], b0), (a_c.at[1], a1), (b_c.at[1], b1), (a_c.at[2], a2), (b_c.at[2], b2))
        for move in copies(pairs, sem):
            move.wait()
        subtract(cols_n, ops, arrived, got, s, a0, b0, s1)


def middle_late(rows_n, cols_n, first, ops, s1, a1, b1, *rest):
    arrived, (s2, got) = rest[: len(ops)], rest[len(ops) :]

    @pl.when(level_of(rows_n) > first + 2)
    def _():
        subtract(cols_n, ops, arrived, got, s1, a1, b1, s2)


def pick(cols_n, ops, kind, arrived, got):
    me = place(cols_n)
    any_hit = me < 0
    for op, ref in zip(ops, arrived):
        hit = one_of(me, [t[0] * cols_n + t[1] for _, t, k, _ in op if k == kind])
        any_hit = any_hit | hit

        @pl.when(hit)
        def _():
            got[...] = ref[...]

    return any_hit


def downs(cols_n, first, rows_n, ops, s2, a2, *rest):
    arrived, (s3, got) = rest[: len(ops)], rest[len(ops) :]

    @pl.when(level_of(rows_n) > first + 2)
    def _():
        subtract(cols_n, ops, arrived, got, s2, a2, None, s3, ("down",))


def finish(rows_n, cols_n, first, ops, f0, f1, f2, s3, b2, *rest):
    arrived, (out, nxt, got, mine, zeros, sem) = rest[: len(ops)], rest[len(ops) :]
    level = level_of(rows_n)
    n = s3.shape[0]
    step = n // 3
    active = level > first + 2
    for t, block in enumerate((f0, f1, f2)):

        @pl.when(level == first + t)
        def _():
            pltpu.make_async_copy(block, out, sem.at[3]).start()

    @pl.when((level < first) | active)
    def _():
        zeros[...] = jnp.zeros(zeros.shape, zeros.dtype)
        pltpu.make_async_copy(zeros, out, sem.at[3]).start()

    @pl.when(jnp.logical_not(active))
    def _():
        mine[...] = jnp.zeros(mine.shape, mine.dtype)
        for k in range(3):
            pltpu.make_async_copy(mine.at[pl.ds(k * step, step)], nxt.at[pl.ds(k * step, step)], sem.at[k]).start()

    @pl.when(active)
    def _():
        pick(cols_n, ops, "left", arrived, got)
        for k in range(3):
            rows = pl.ds(k * step, step)
            mine[rows] = s3[rows] - dot(got[rows], b2[...])
            pltpu.make_async_copy(mine.at[rows], nxt.at[rows], sem.at[k]).start()

    for k in range(3):
        pltpu.make_async_copy(mine.at[pl.ds(k * step, step)], nxt.at[pl.ds(k * step, step)], sem.at[k]).wait()
    pltpu.make_async_copy(zeros, out, sem.at[3]).wait()


def relay(cols_n, choices, own, *rest):
    *arrived, out = rest
    me = place(cols_n)
    hit = me < 0
    for ids, ref in zip(choices, arrived):
        mine = one_of(me, ids)
        hit = hit | mine

        @pl.when(mine)
        def _():
            out[...] = ref[...]

    @pl.when(jnp.logical_not(hit))
    def _():
        out[...] = own[...]


def spread(ops, cols_n, own, name, call):
    arrived = []
    for k, op in enumerate(ops):
        value = own
        earlier = sorted({f for *_, f in op if f is not None})
        if earlier:
            choices = [[s[0] * cols_n + s[1] for s, _, _, f in op if f == e] for e in earlier]
            (value,) = call(
                functools.partial(relay, cols_n, choices),
                [],
                [own, *[arrived[e] for e in earlier]],
                [jax.ShapeDtypeStruct(own.shape, own.dtype)],
                [],
                f"relay_{name}{k}",
            )
        pairs = [(s[0] * cols_n + s[1], t[0] * cols_n + t[1]) for s, t, _, _ in op]
        arrived.append(move(value, pairs))
    return arrived


def move(value, pairs):
    return lax.ppermute(value, AXES, pairs)


def solution(mesh):
    rows_n, cols_n = mesh.shape["row"], mesh.shape["col"]
    first = (rows_n + cols_n) // 2 - 2
    offset = first - rows_n + 1
    ops0 = plan(rows_n, cols_n, offset, 3, 3)
    ops1 = plan(rows_n, cols_n, offset + 1, 2, 2)
    ops2 = plan(rows_n, cols_n, offset + 2, 1, 1)

    def owners(t):
        return [(i, i + offset + t) for i in range(rows_n) if 0 <= i + offset + t < cols_n]

    def up(t, far):
        return [(i * cols_n + j, (i - far) * cols_n + j) for i, j in owners(t) if i >= far]

    def right(t, far):
        return [(i * cols_n + j, i * cols_n + j + far) for i, j in owners(t) if j + far < cols_n]

    def shards(rhs, a_c, b_c, u, v, a_vals, b_vals):
        n = rhs.shape[0]
        half, full = jnp.bfloat16, jnp.float32
        square = jax.ShapeDtypeStruct((n, n), half)
        wide, tall = jax.ShapeDtypeStruct((n, 3 * n), half), jax.ShapeDtypeStruct((3 * n, n), half)
        state = jax.ShapeDtypeStruct((n, n), full)
        loads = [pltpu.VMEM((n, n), full)] * 3 + [pltpu.VMEM((n,), full)] * 2
        basis_work = [pltpu.VMEM((n, 3 * n), half)] * 2 + [pltpu.VMEM((3 * n, n), half), pltpu.VMEM((n, 3 * n), half), pltpu.VMEM((n, n), full)]
        work = [pltpu.VMEM((n, 3 * n), half), pltpu.VMEM((3 * n, n), half)]

        def call(kernel, far, near, outs, scratch, name):
            ins = [pltpu.with_memory_space_constraint(x, pltpu.HBM) for x in far] + list(near)
            return pl.pallas_call(
                kernel,
                out_shape=outs,
                in_specs=[FAR_SPEC] * len(far) + [VMEM_SPEC] * len(near),
                out_specs=[FAR_SPEC if name == "finish" else VMEM_SPEC] * len(outs),
                scratch_shapes=scratch,
                compiler_params=pltpu.CompilerParams(vmem_limit_bytes=24 << 20),
            )(*ins)

        basis_shapes = [wide, wide, tall, wide, state]
        (f0,) = call(
            functools.partial(begin, rows_n, first),
            [rhs, u, v, a_vals, b_vals],
            [],
            [square],
            loads + basis_work + work + [pltpu.SemaphoreType.DMA((5,))],
            "begin",
        )
        down = move(f0, up(0, 1))
        left = move(f0, right(0, 1))
        down_far = move(f0, up(0, 2))
        direct, on_chip = [], []
        for i, j in owners(0):
            if j + 2 < cols_n:
                source, target = (j, direct) if j % 2 == 0 else (j + 1, on_chip)
                target.append((i * cols_n + source, i * cols_n + j + 2))
        left_far = [move(f0, direct), move(left, on_chip)]
        far0 = spread(ops0, cols_n, f0, "a", call)
        *basis, s, ca, cb = call(
            functools.partial(prepare, rows_n, first),
            [rhs, a_c, b_c, u, v, a_vals, b_vals],
            [],
            basis_shapes + [state, square, square],
            loads[1:] + [pltpu.SemaphoreType.DMA((7,))],
            "prepare",
        )
        (f1,) = call(
            functools.partial(second, rows_n, first),
            [],
            [down, left, *basis, s, ca, cb],
            [square],
            work,
            "second",
        )
        down = move(f1, up(1, 1))
        left = move(f1, right(1, 1))
        s1, a1, b1 = call(
            functools.partial(third_early, rows_n, first),
            [rhs, a_c, b_c],
            [down_far, *left_far],
            [state, square, square],
            [pltpu.VMEM((n, n), half)] * 2 + [pltpu.SemaphoreType.DMA((5,))],
            "third_early",
        )
        far1 = spread(ops1, cols_n, f1, "b", call)
        (f2,) = call(
            functools.partial(third, rows_n, first),
            [],
            [down, left, *basis, s1, a1, b1],
            [square],
            work,
            "third",
        )
        s1, a1, b1, a2, b2 = call(
            functools.partial(middle, rows_n, cols_n, first, ops0),
            [rhs, a_c, b_c],
            far0,
            [state] + [square] * 4,
            [pltpu.VMEM((n, n), full)] + [pltpu.VMEM((n, n), half)] * 3 + [pltpu.SemaphoreType.DMA((7,))],
            "middle",
        )
        (s2,) = call(
            functools.partial(middle_late, rows_n, cols_n, first, ops1),
            [],
            [s1, a1, b1, *far1],
            [state],
            [pltpu.VMEM((n, n), half)],
            "middle_late",
        )
        lasts = spread(ops2, cols_n, f2, "c", call)
        sent = [k for k, op in enumerate(ops2) if any(kind == "down" for _, _, kind, _ in op)]
        (s3,) = call(
            functools.partial(downs, cols_n, first, rows_n, [ops2[k] for k in sent]),
            [],
            [s2, a2, *[lasts[k] for k in sent]],
            [state],
            [pltpu.VMEM((n, n), half)],
            "downs",
        )
        return call(
            functools.partial(finish, rows_n, cols_n, first, ops2),
            [],
            [f0, f1, f2, s3, b2, *lasts],
            [square, state],
            [pltpu.VMEM((n, n), half), pltpu.VMEM((n, n), full), pltpu.VMEM((n, n), half), pltpu.SemaphoreType.DMA((4,))],
            "finish",
        )

    placed = (
        P("row", "col"),
        P(None, "row", "col"),
        P(None, "row", "col"),
        P("row", None),
        P("col", None),
        P("row"),
        P("col"),
    )
    return jax.shard_map(
        shards,
        mesh=mesh,
        in_specs=placed,
        out_specs=(P("row", "col"), P("row", "col")),
        check_vma=False,
    )
```

```python
import functools

import jax
import jax.numpy as jnp
from jax import lax
from jax.experimental import pallas as pl
from jax.experimental.pallas import tpu as pltpu
from jax.sharding import PartitionSpec as P


AXES = ("row", "col")
VMEM_SPEC = pl.BlockSpec(memory_space=pltpu.VMEM)
FAR_SPEC = pl.BlockSpec(memory_space=pltpu.HBM)


def plan(rows_n, cols_n, offset, gap, up_gap):
    rights, ups, last = [], [], []
    for i in range(rows_n):
        m = i + offset
        if 0 <= m < cols_n:
            targets = range(m + gap, cols_n)
            for chip in sorted({j // 2 for j in targets}, reverse=True):
                some = [(i, j) for j in targets if j // 2 == chip]
                (last if chip == m // 2 else rights).append(((i, m), some, "left"))
            ups += [((i, m), [(k, m)], "down") for k in range(i - up_gap + 1)]
    todo = rights + ups + last
    ops, forwards = [], []
    while todo:
        used_from, used_to, op = set(), set(), []
        waiting = {targets[0] for _, targets, kind in todo if kind == "down"}
        for item in list(todo):
            source, targets, kind = item
            for target in sorted(targets, key=lambda t: t in waiting):
                if source not in used_from and target not in used_to:
                    used_from.add(source)
                    used_to.add(target)
                    op.append((source, target, kind, None))
                    todo.remove(item)
                    forwards += [(target, other, kind, len(ops)) for other in targets if other != target]
                    break
        ops.append(op)
    return ops + [forwards] if forwards else ops


def one_of(me, ids):
    hit = me < 0
    for each in sorted(ids):
        hit = hit | (me == each)
    return hit


def place(cols_n):
    return lax.axis_index("row") * cols_n + lax.axis_index("col")


def level_of(rows_n):
    return rows_n - 1 - lax.axis_index("row") + lax.axis_index("col")


def dot(a, b):
    return lax.dot_general(a, b, (((1,), (0,)), ((), ())), preferred_element_type=jnp.float32)


def split(x):
    high = x.astype(jnp.bfloat16)
    return high, (x - high.astype(jnp.float32)).astype(jnp.bfloat16)


def put_left(ref, pair):
    n = pair[0].shape[1]
    ref[:, 0:n] = pair[0]
    ref[:, n : 2 * n] = pair[0]
    ref[:, 2 * n : 3 * n] = pair[1]


def put_right(ref, pair):
    n = pair[0].shape[0]
    ref[0:n] = pair[0]
    ref[n : 2 * n] = pair[1]
    ref[2 * n : 3 * n] = pair[0]


def dot_t(a, b):
    return lax.dot_general(a, b, (((1,), (1,)), ((), ())), preferred_element_type=jnp.float32)


def solve(state, uk, utk, vk, vl, inverse, lhs, mid):
    put_left(lhs, split(state))
    part = dot(lhs[...], vk[...])
    put_right(mid, split(part))
    part = dot(utk[...], mid[...]) * inverse[...]
    put_left(lhs, split(part))
    part = dot_t(lhs[...], vl[...])
    put_right(mid, split(part))
    return dot(uk[...], mid[...]).astype(jnp.bfloat16)


def put_lanes(ref, pair):
    n = pair[0].shape[1]
    ref[:, 0:n] = pair[0]
    ref[:, n : 2 * n] = pair[1]
    ref[:, 2 * n : 3 * n] = pair[0]


def set_inverse(inverse, av, bv):
    n = inverse.shape[0]
    alpha = jnp.transpose(jnp.broadcast_to(av[...][None, :], (128, n)))
    beta = bv[...][None, :]
    for c in range(0, n, 128):
        inverse[:, c : c + 128] = 1.0 / (alpha + beta[:, c : c + 128])


def set_right_basis(v, vk, vl):
    pair = split(v[...])
    put_right(vk, pair)
    put_lanes(vl, pair)


def set_left_basis(u, uk, utk):
    high, low = split(u[...])
    put_left(uk, (high, low))
    put_left(utk, (high.T, low.T))


def copies(pairs, sem):
    moves = [pltpu.make_async_copy(source, target, sem.at[n]) for n, (source, target) in enumerate(pairs)]
    for move in moves:
        move.start()
    return moves


def begin(rows_n, first, rhs, u_far, v_far, a_vals, b_vals, f0, s, u, v, av, bv, uk, utk, vk, vl, inverse, lhs, mid, sem):
    @pl.when(level_of(rows_n) == first)
    def _():
        moves = copies(((v_far, v), (rhs, s), (u_far, u), (a_vals, av), (b_vals, bv)), sem)
        moves[0].wait()
        set_right_basis(v, vk, vl)
        for move in moves[1:]:
            move.wait()
        set_left_basis(u, uk, utk)
        set_inverse(inverse, av, bv)
        f0[...] = solve(s[...], uk, utk, vk, vl, inverse, lhs, mid)


def prepare(rows_n, first, rhs, a_c, b_c, u_far, v_far, a_vals, b_vals, uk, utk, vk, vl, inverse, s, a0, b0, a1, b1, u, v, av, bv, sem):
    level = level_of(rows_n)

    @pl.when((level > first) & (level <= first + 2))
    def _():
        moves = copies(((v_far, v), (u_far, u), (a_vals, av), (b_vals, bv), (rhs, s), (a_c.at[0], a0), (b_c.at[0], b0), (a_c.at[1], a1), (b_c.at[1], b1)), sem)
        moves[0].wait()
        set_right_basis(v, vk, vl)
        moves[1].wait()
        set_left_basis(u, uk, utk)
        moves[2].wait()
        moves[3].wait()
        set_inverse(inverse, av, bv)
        for move in moves[4:]:
            move.wait()


def second(rows_n, first, down, left, uk, utk, vk, vl, inverse, s, ca, cb, f1, lhs, mid):
    @pl.when(level_of(rows_n) == first + 1)
    def _():
        state = s[...] - (dot(ca[...], down[...]) + dot(left[...], cb[...]))
        f1[...] = solve(state, uk, utk, vk, vl, inverse, lhs, mid)


def third_early(rows_n, first, down, direct, on_chip, s, a0, b0, s1):
    even = lax.rem(lax.axis_index("col"), 2) == 0

    @pl.when(level_of(rows_n) == first + 2)
    def _():
        left = jnp.where(even, direct[...], on_chip[...])
        s1[...] = s[...] - (dot(a0[...], down[...]) + dot(left, b0[...]))


def third(rows_n, first, down, left, uk, utk, vk, vl, inverse, s1, a1, b1, f2, lhs, mid):
    @pl.when(level_of(rows_n) == first + 2)
    def _():
        state = s1[...] - (dot(a1[...], down[...]) + dot(left[...], b1[...]))
        f2[...] = solve(state, uk, utk, vk, vl, inverse, lhs, mid)


def subtract(cols_n, ops, arrived, got, state, coup_a, coup_b, out, kinds=("down", "left")):
    out[...] = state[...]
    for kind in kinds:
        hits = pick(cols_n, ops, kind, arrived, got)

        @pl.when(hits)
        def _():
            out[...] -= dot(got[...], coup_b[...]) if kind == "left" else dot(coup_a[...], got[...])


def middle(rows_n, cols_n, first, ops, rhs, a_c, b_c, *rest):
    arrived, (s1, a1, b1, a2, b2, s, a0, b0, got, sem) = rest[: len(ops)], rest[len(ops) :]

    @pl.when(level_of(rows_n) > first + 2)
    def _():
        pairs = ((rhs, s), (a_c.at[0], a0), (b_c.at[0], b0), (a_c.at[1], a1), (b_c.at[1], b1), (a_c.at[2], a2), (b_c.at[2], b2))
        for move in copies(pairs, sem):
            move.wait()
        subtract(cols_n, ops, arrived, got, s, a0, b0, s1)


def middle_late(rows_n, cols_n, first, ops, s1, a1, b1, *rest):
    arrived, (s2, got) = rest[: len(ops)], rest[len(ops) :]

    @pl.when(level_of(rows_n) > first + 2)
    def _():
        subtract(cols_n, ops, arrived, got, s1, a1, b1, s2)


def pick(cols_n, ops, kind, arrived, got):
    me = place(cols_n)
    any_hit = me < 0
    for op, ref in zip(ops, arrived):
        hit = one_of(me, [t[0] * cols_n + t[1] for _, t, k, _ in op if k == kind])
        any_hit = any_hit | hit

        @pl.when(hit)
        def _():
            got[...] = ref[...]

    return any_hit


def downs(cols_n, first, rows_n, ops, s2, a2, *rest):
    arrived, (s3, got) = rest[: len(ops)], rest[len(ops) :]

    @pl.when(level_of(rows_n) > first + 2)
    def _():
        subtract(cols_n, ops, arrived, got, s2, a2, None, s3, ("down",))


def finish(rows_n, cols_n, first, ops, f0, f1, f2, s3, b2, *rest):
    arrived, (out, nxt, got, mine, zeros, sem) = rest[: len(ops)], rest[len(ops) :]
    level = level_of(rows_n)
    n = s3.shape[0]
    step = n // 3
    active = level > first + 2
    for t, block in enumerate((f0, f1, f2)):

        @pl.when(level == first + t)
        def _():
            pltpu.make_async_copy(block, out, sem.at[3]).start()

    @pl.when((level < first) | active)
    def _():
        zeros[...] = jnp.zeros(zeros.shape, zeros.dtype)
        pltpu.make_async_copy(zeros, out, sem.at[3]).start()

    @pl.when(jnp.logical_not(active))
    def _():
        mine[...] = jnp.zeros(mine.shape, mine.dtype)
        for k in range(3):
            pltpu.make_async_copy(mine.at[pl.ds(k * step, step)], nxt.at[pl.ds(k * step, step)], sem.at[k]).start()

    @pl.when(active)
    def _():
        pick(cols_n, ops, "left", arrived, got)
        for k in range(3):
            rows = pl.ds(k * step, step)
            mine[rows] = s3[rows] - dot(got[rows], b2[...])
            pltpu.make_async_copy(mine.at[rows], nxt.at[rows], sem.at[k]).start()

    for k in range(3):
        pltpu.make_async_copy(mine.at[pl.ds(k * step, step)], nxt.at[pl.ds(k * step, step)], sem.at[k]).wait()
    pltpu.make_async_copy(zeros, out, sem.at[3]).wait()


def relay(cols_n, choices, own, *rest):
    *arrived, out = rest
    me = place(cols_n)
    hit = me < 0
    for ids, ref in zip(choices, arrived):
        mine = one_of(me, ids)
        hit = hit | mine

        @pl.when(mine)
        def _():
            out[...] = ref[...]

    @pl.when(jnp.logical_not(hit))
    def _():
        out[...] = own[...]


def spread(ops, cols_n, own, name, call):
    arrived = []
    for k, op in enumerate(ops):
        value = own
        earlier = sorted({f for *_, f in op if f is not None})
        if earlier:
            choices = [[s[0] * cols_n + s[1] for s, _, _, f in op if f == e] for e in earlier]
            (value,) = call(
                functools.partial(relay, cols_n, choices),
                [],
                [own, *[arrived[e] for e in earlier]],
                [jax.ShapeDtypeStruct(own.shape, own.dtype)],
                [],
                f"relay_{name}{k}",
            )
        pairs = [(s[0] * cols_n + s[1], t[0] * cols_n + t[1]) for s, t, _, _ in op]
        arrived.append(move(value, pairs))
    return arrived


def move(value, pairs):
    return lax.ppermute(value, AXES, pairs)


def solution(mesh):
    rows_n, cols_n = mesh.shape["row"], mesh.shape["col"]
    first = (rows_n + cols_n) // 2 - 2
    offset = first - rows_n + 1
    ops0 = plan(rows_n, cols_n, offset, 3, 3)
    ops1 = plan(rows_n, cols_n, offset + 1, 2, 2)
    ops2 = plan(rows_n, cols_n, offset + 2, 1, 1)

    def owners(t):
        return [(i, i + offset + t) for i in range(rows_n) if 0 <= i + offset + t < cols_n]

    def up(t, far):
        return [(i * cols_n + j, (i - far) * cols_n + j) for i, j in owners(t) if i >= far]

    def right(t, far):
        return [(i * cols_n + j, i * cols_n + j + far) for i, j in owners(t) if j + far < cols_n]

    def shards(rhs, a_c, b_c, u, v, a_vals, b_vals):
        n = rhs.shape[0]
        half, full = jnp.bfloat16, jnp.float32
        square = jax.ShapeDtypeStruct((n, n), half)
        wide, tall = jax.ShapeDtypeStruct((n, 3 * n), half), jax.ShapeDtypeStruct((3 * n, n), half)
        state = jax.ShapeDtypeStruct((n, n), full)
        loads = [pltpu.VMEM((n, n), full)] * 3 + [pltpu.VMEM((n,), full)] * 2
        basis_work = [pltpu.VMEM((n, 3 * n), half)] * 2 + [pltpu.VMEM((3 * n, n), half), pltpu.VMEM((n, 3 * n), half), pltpu.VMEM((n, n), full)]
        work = [pltpu.VMEM((n, 3 * n), half), pltpu.VMEM((3 * n, n), half)]

        def call(kernel, far, near, outs, scratch, name):
            ins = [pltpu.with_memory_space_constraint(x, pltpu.HBM) for x in far] + list(near)
            return pl.pallas_call(
                kernel,
                out_shape=outs,
                in_specs=[FAR_SPEC] * len(far) + [VMEM_SPEC] * len(near),
                out_specs=[FAR_SPEC if name == "finish" else VMEM_SPEC] * len(outs),
                scratch_shapes=scratch,
                compiler_params=pltpu.CompilerParams(vmem_limit_bytes=24 << 20),
            )(*ins)

        basis_shapes = [wide, wide, tall, wide, state]
        (f0,) = call(
            functools.partial(begin, rows_n, first),
            [rhs, u, v, a_vals, b_vals],
            [],
            [square],
            loads + basis_work + work + [pltpu.SemaphoreType.DMA((5,))],
            "begin",
        )
        down = move(f0, up(0, 1))
        left = move(f0, right(0, 1))
        down_far = move(f0, up(0, 2))
        direct, on_chip = [], []
        for i, j in owners(0):
            if j + 2 < cols_n:
                source, target = (j, direct) if j % 2 == 0 else (j + 1, on_chip)
                target.append((i * cols_n + source, i * cols_n + j + 2))
        left_far = [move(f0, direct), move(left, on_chip)]
        far0 = spread(ops0, cols_n, f0, "a", call)
        *basis, s, a0, b0, a1, b1 = call(
            functools.partial(prepare, rows_n, first),
            [rhs, a_c, b_c, u, v, a_vals, b_vals],
            [],
            basis_shapes + [state] + [square] * 4,
            loads[1:] + [pltpu.SemaphoreType.DMA((9,))],
            "prepare",
        )
        (f1,) = call(
            functools.partial(second, rows_n, first),
            [],
            [down, left, *basis, s, a0, b0],
            [square],
            work,
            "second",
        )
        down = move(f1, up(1, 1))
        left = move(f1, right(1, 1))
        (s1,) = call(
            functools.partial(third_early, rows_n, first),
            [],
            [down_far, *left_far, s, a0, b0],
            [state],
            [],
            "third_early",
        )
        far1 = spread(ops1, cols_n, f1, "b", call)
        (f2,) = call(
            functools.partial(third, rows_n, first),
            [],
            [down, left, *basis, s1, a1, b1],
            [square],
            work,
            "third",
        )
        s1, a1, b1, a2, b2 = call(
            functools.partial(middle, rows_n, cols_n, first, ops0),
            [rhs, a_c, b_c],
            far0,
            [state] + [square] * 4,
            [pltpu.VMEM((n, n), full)] + [pltpu.VMEM((n, n), half)] * 3 + [pltpu.SemaphoreType.DMA((7,))],
            "middle",
        )
        (s2,) = call(
            functools.partial(middle_late, rows_n, cols_n, first, ops1),
            [],
            [s1, a1, b1, *far1],
            [state],
            [pltpu.VMEM((n, n), half)],
            "middle_late",
        )
        lasts = spread(ops2, cols_n, f2, "c", call)
        sent = [k for k, op in enumerate(ops2) if any(kind == "down" for _, _, kind, _ in op)]
        (s3,) = call(
            functools.partial(downs, cols_n, first, rows_n, [ops2[k] for k in sent]),
            [],
            [s2, a2, *[lasts[k] for k in sent]],
            [state],
            [pltpu.VMEM((n, n), half)],
            "downs",
        )
        return call(
            functools.partial(finish, rows_n, cols_n, first, ops2),
            [],
            [f0, f1, f2, s3, b2, *lasts],
            [square, state],
            [pltpu.VMEM((n, n), half), pltpu.VMEM((n, n), full), pltpu.VMEM((n, n), half), pltpu.SemaphoreType.DMA((4,))],
            "finish",
        )

    placed = (
        P("row", "col"),
        P(None, "row", "col"),
        P(None, "row", "col"),
        P("row", None),
        P("col", None),
        P("row"),
        P("col"),
    )
    return jax.shard_map(
        shards,
        mesh=mesh,
        in_specs=placed,
        out_specs=(P("row", "col"), P("row", "col")),
        check_vma=False,
    )
```

```python
import functools

import jax
import jax.numpy as jnp
from jax import lax
from jax.experimental import pallas as pl
from jax.experimental.pallas import tpu as pltpu
from jax.sharding import PartitionSpec as P


AXES = ("row", "col")
VMEM_SPEC = pl.BlockSpec(memory_space=pltpu.VMEM)
FAR_SPEC = pl.BlockSpec(memory_space=pltpu.HBM)


def plan(rows_n, cols_n, offset, gap, up_gap):
    rights, ups, last = [], [], []
    for i in range(rows_n):
        m = i + offset
        if 0 <= m < cols_n:
            targets = range(m + gap, cols_n)
            for chip in sorted({j // 2 for j in targets}, reverse=True):
                some = [(i, j) for j in targets if j // 2 == chip]
                (last if chip == m // 2 else rights).append(((i, m), some, "left"))
            ups += [((i, m), [(k, m)], "down") for k in range(i - up_gap + 1)]
    todo = rights + ups + last
    ops, forwards = [], []
    while todo:
        used_from, used_to, op = set(), set(), []
        waiting = {targets[0] for _, targets, kind in todo if kind == "down"}
        for item in list(todo):
            source, targets, kind = item
            for target in sorted(targets, key=lambda t: t in waiting):
                if source not in used_from and target not in used_to:
                    used_from.add(source)
                    used_to.add(target)
                    op.append((source, target, kind, None))
                    todo.remove(item)
                    forwards += [(target, other, kind, len(ops)) for other in targets if other != target]
                    break
        ops.append(op)
    return ops + [forwards] if forwards else ops


def one_of(me, ids):
    hit = me < 0
    for each in sorted(ids):
        hit = hit | (me == each)
    return hit


def place(cols_n):
    return lax.axis_index("row") * cols_n + lax.axis_index("col")


def level_of(rows_n):
    return rows_n - 1 - lax.axis_index("row") + lax.axis_index("col")


def dot(a, b):
    return lax.dot_general(a, b, (((1,), (0,)), ((), ())), preferred_element_type=jnp.float32)


def split(x):
    high = x.astype(jnp.bfloat16)
    return high, (x - high.astype(jnp.float32)).astype(jnp.bfloat16)


def put_left(ref, pair):
    n = pair[0].shape[1]
    ref[:, 0:n] = pair[0]
    ref[:, n : 2 * n] = pair[0]
    ref[:, 2 * n : 3 * n] = pair[1]


def put_right(ref, pair):
    n = pair[0].shape[0]
    ref[0:n] = pair[0]
    ref[n : 2 * n] = pair[1]
    ref[2 * n : 3 * n] = pair[0]


def dot_t(a, b):
    return lax.dot_general(a, b, (((1,), (1,)), ((), ())), preferred_element_type=jnp.float32)


def solve(state, uk, utk, vk, vl, inverse, lhs, mid):
    put_left(lhs, split(state))
    part = dot(lhs[...], vk[...])
    put_right(mid, split(part))
    part = dot(utk[...], mid[...]) * inverse[...]
    put_left(lhs, split(part))
    part = dot_t(lhs[...], vl[...])
    put_right(mid, split(part))
    return dot(uk[...], mid[...]).astype(jnp.bfloat16)


def put_lanes(ref, pair):
    n = pair[0].shape[1]
    ref[:, 0:n] = pair[0]
    ref[:, n : 2 * n] = pair[1]
    ref[:, 2 * n : 3 * n] = pair[0]


def set_inverse(inverse, av, bv):
    n = inverse.shape[0]
    alpha = jnp.transpose(jnp.broadcast_to(av[...][None, :], (128, n)))
    beta = bv[...][None, :]
    for c in range(0, n, 128):
        inverse[:, c : c + 128] = 1.0 / (alpha + beta[:, c : c + 128])


def set_right_basis(v, vk, vl):
    pair = split(v[...])
    put_right(vk, pair)
    put_lanes(vl, pair)


def set_left_basis(u, uk, utk):
    high, low = split(u[...])
    put_left(uk, (high, low))
    put_left(utk, (high.T, low.T))


def copies(pairs, sem):
    moves = [pltpu.make_async_copy(source, target, sem.at[n]) for n, (source, target) in enumerate(pairs)]
    for move in moves:
        move.start()
    return moves


def begin(rows_n, first, rhs, u_far, v_far, a_vals, b_vals, f0, s, u, v, av, bv, uk, utk, vk, vl, inverse, lhs, mid, sem):
    @pl.when(level_of(rows_n) == first)
    def _():
        moves = copies(((v_far, v), (rhs, s), (u_far, u), (a_vals, av), (b_vals, bv)), sem)
        moves[0].wait()
        set_right_basis(v, vk, vl)
        for move in moves[1:]:
            move.wait()
        set_left_basis(u, uk, utk)
        set_inverse(inverse, av, bv)
        f0[...] = solve(s[...], uk, utk, vk, vl, inverse, lhs, mid)


def prepare(rows_n, first, rhs, a_c, b_c, u_far, v_far, a_vals, b_vals, uk, utk, vk, vl, inverse, s, a0, b0, a1, b1, u, v, av, bv, sem):
    level = level_of(rows_n)

    @pl.when((level > first) & (level <= first + 2))
    def _():
        moves = copies(((v_far, v), (u_far, u), (a_vals, av), (b_vals, bv), (rhs, s), (a_c.at[0], a0), (b_c.at[0], b0), (a_c.at[1], a1), (b_c.at[1], b1)), sem)
        moves[0].wait()
        set_right_basis(v, vk, vl)
        moves[1].wait()
        set_left_basis(u, uk, utk)
        moves[2].wait()
        moves[3].wait()
        set_inverse(inverse, av, bv)
        for move in moves[4:]:
            move.wait()


def second(rows_n, first, down, left, uk, utk, vk, vl, inverse, s, ca, cb, f1, lhs, mid):
    @pl.when(level_of(rows_n) == first + 1)
    def _():
        state = s[...] - (dot(ca[...], down[...]) + dot(left[...], cb[...]))
        f1[...] = solve(state, uk, utk, vk, vl, inverse, lhs, mid)


def third_early(rows_n, first, down, left, s, a0, b0, s1):
    @pl.when(level_of(rows_n) == first + 2)
    def _():
        s1[...] = s[...] - (dot(a0[...], down[...]) + dot(left[...], b0[...]))


def third(rows_n, first, down, left, uk, utk, vk, vl, inverse, s1, a1, b1, f2, lhs, mid):
    @pl.when(level_of(rows_n) == first + 2)
    def _():
        state = s1[...] - (dot(a1[...], down[...]) + dot(left[...], b1[...]))
        f2[...] = solve(state, uk, utk, vk, vl, inverse, lhs, mid)


def subtract(cols_n, ops, arrived, got, state, coup_a, coup_b, out, kinds=("down", "left")):
    out[...] = state[...]
    for kind in kinds:
        hits = pick(cols_n, ops, kind, arrived, got)

        @pl.when(hits)
        def _():
            out[...] -= dot(got[...], coup_b[...]) if kind == "left" else dot(coup_a[...], got[...])


def middle(rows_n, cols_n, first, ops, rhs, a_c, b_c, *rest):
    arrived, (s1, a1, b1, a2, b2, s, a0, b0, got, sem) = rest[: len(ops)], rest[len(ops) :]

    @pl.when(level_of(rows_n) > first + 2)
    def _():
        pairs = ((rhs, s), (a_c.at[0], a0), (b_c.at[0], b0), (a_c.at[1], a1), (b_c.at[1], b1), (a_c.at[2], a2), (b_c.at[2], b2))
        for move in copies(pairs, sem):
            move.wait()
        subtract(cols_n, ops, arrived, got, s, a0, b0, s1)


def middle_late(rows_n, cols_n, first, ops, s1, a1, b1, *rest):
    arrived, (s2, got) = rest[: len(ops)], rest[len(ops) :]

    @pl.when(level_of(rows_n) > first + 2)
    def _():
        subtract(cols_n, ops, arrived, got, s1, a1, b1, s2)


def pick(cols_n, ops, kind, arrived, got):
    me = place(cols_n)
    any_hit = me < 0
    for op, ref in zip(ops, arrived):
        hit = one_of(me, [t[0] * cols_n + t[1] for _, t, k, _ in op if k == kind])
        any_hit = any_hit | hit

        @pl.when(hit)
        def _():
            got[...] = ref[...]

    return any_hit


def downs(cols_n, first, rows_n, ops, s2, a2, *rest):
    arrived, (s3, got) = rest[: len(ops)], rest[len(ops) :]

    @pl.when(level_of(rows_n) > first + 2)
    def _():
        subtract(cols_n, ops, arrived, got, s2, a2, None, s3, ("down",))


def finish(rows_n, cols_n, first, ops, f0, f1, f2, s3, b2, *rest):
    arrived, (out, nxt, got, mine, zeros, sem) = rest[: len(ops)], rest[len(ops) :]
    level = level_of(rows_n)
    n = s3.shape[0]
    step = n // 3
    active = level > first + 2
    for t, block in enumerate((f0, f1, f2)):

        @pl.when(level == first + t)
        def _():
            pltpu.make_async_copy(block, out, sem.at[3]).start()

    @pl.when((level < first) | active)
    def _():
        zeros[...] = jnp.zeros(zeros.shape, zeros.dtype)
        pltpu.make_async_copy(zeros, out, sem.at[3]).start()

    @pl.when(jnp.logical_not(active))
    def _():
        mine[...] = jnp.zeros(mine.shape, mine.dtype)
        for k in range(3):
            pltpu.make_async_copy(mine.at[pl.ds(k * step, step)], nxt.at[pl.ds(k * step, step)], sem.at[k]).start()

    @pl.when(active)
    def _():
        pick(cols_n, ops, "left", arrived, got)
        for k in range(3):
            rows = pl.ds(k * step, step)
            mine[rows] = s3[rows] - dot(got[rows], b2[...])
            pltpu.make_async_copy(mine.at[rows], nxt.at[rows], sem.at[k]).start()

    for k in range(3):
        pltpu.make_async_copy(mine.at[pl.ds(k * step, step)], nxt.at[pl.ds(k * step, step)], sem.at[k]).wait()
    pltpu.make_async_copy(zeros, out, sem.at[3]).wait()


def relay(cols_n, choices, own, *rest):
    *arrived, out = rest
    me = place(cols_n)
    hit = me < 0
    for ids, ref in zip(choices, arrived):
        mine = one_of(me, ids)
        hit = hit | mine

        @pl.when(mine)
        def _():
            out[...] = ref[...]

    @pl.when(jnp.logical_not(hit))
    def _():
        out[...] = own[...]


def spread(ops, cols_n, own, name, call):
    arrived = []
    for k, op in enumerate(ops):
        value = own
        earlier = sorted({f for *_, f in op if f is not None})
        if earlier:
            choices = [[s[0] * cols_n + s[1] for s, _, _, f in op if f == e] for e in earlier]
            (value,) = call(
                functools.partial(relay, cols_n, choices),
                [],
                [own, *[arrived[e] for e in earlier]],
                [jax.ShapeDtypeStruct(own.shape, own.dtype)],
                [],
                f"relay_{name}{k}",
            )
        pairs = [(s[0] * cols_n + s[1], t[0] * cols_n + t[1]) for s, t, _, _ in op]
        arrived.append(move(value, pairs))
    return arrived


def move(value, pairs):
    return lax.ppermute(value, AXES, pairs)


def solution(mesh):
    rows_n, cols_n = mesh.shape["row"], mesh.shape["col"]
    first = (rows_n + cols_n) // 2 - 2
    offset = first - rows_n + 1
    ops0 = plan(rows_n, cols_n, offset, 3, 3)
    ops1 = plan(rows_n, cols_n, offset + 1, 2, 2)
    ops2 = plan(rows_n, cols_n, offset + 2, 1, 1)

    def owners(t):
        return [(i, i + offset + t) for i in range(rows_n) if 0 <= i + offset + t < cols_n]

    def up(t, far):
        return [(i * cols_n + j, (i - far) * cols_n + j) for i, j in owners(t) if i >= far]

    def right(t, far):
        return [(i * cols_n + j, i * cols_n + j + far) for i, j in owners(t) if j + far < cols_n]

    def shards(rhs, a_c, b_c, u, v, a_vals, b_vals):
        n = rhs.shape[0]
        half, full = jnp.bfloat16, jnp.float32
        square = jax.ShapeDtypeStruct((n, n), half)
        wide, tall = jax.ShapeDtypeStruct((n, 3 * n), half), jax.ShapeDtypeStruct((3 * n, n), half)
        state = jax.ShapeDtypeStruct((n, n), full)
        loads = [pltpu.VMEM((n, n), full)] * 3 + [pltpu.VMEM((n,), full)] * 2
        basis_work = [pltpu.VMEM((n, 3 * n), half)] * 2 + [pltpu.VMEM((3 * n, n), half), pltpu.VMEM((n, 3 * n), half), pltpu.VMEM((n, n), full)]
        work = [pltpu.VMEM((n, 3 * n), half), pltpu.VMEM((3 * n, n), half)]

        def call(kernel, far, near, outs, scratch, name):
            ins = [pltpu.with_memory_space_constraint(x, pltpu.HBM) for x in far] + list(near)
            return pl.pallas_call(
                kernel,
                out_shape=outs,
                in_specs=[FAR_SPEC] * len(far) + [VMEM_SPEC] * len(near),
                out_specs=[FAR_SPEC if name == "finish" else VMEM_SPEC] * len(outs),
                scratch_shapes=scratch,
                compiler_params=pltpu.CompilerParams(vmem_limit_bytes=24 << 20),
            )(*ins)

        basis_shapes = [wide, wide, tall, wide, state]
        (f0,) = call(
            functools.partial(begin, rows_n, first),
            [rhs, u, v, a_vals, b_vals],
            [],
            [square],
            loads + basis_work + work + [pltpu.SemaphoreType.DMA((5,))],
            "begin",
        )
        down = move(f0, up(0, 1))
        left = move(f0, right(0, 1))
        down_far = move(f0, up(0, 2))
        left_far = move(f0, right(0, 2))
        far0 = spread(ops0, cols_n, f0, "a", call)
        *basis, s, a0, b0, a1, b1 = call(
            functools.partial(prepare, rows_n, first),
            [rhs, a_c, b_c, u, v, a_vals, b_vals],
            [],
            basis_shapes + [state] + [square] * 4,
            loads[1:] + [pltpu.SemaphoreType.DMA((9,))],
            "prepare",
        )
        (f1,) = call(
            functools.partial(second, rows_n, first),
            [],
            [down, left, *basis, s, a0, b0],
            [square],
            work,
            "second",
        )
        down = move(f1, up(1, 1))
        left = move(f1, right(1, 1))
        (s1,) = call(
            functools.partial(third_early, rows_n, first),
            [],
            [down_far, left_far, s, a0, b0],
            [state],
            [],
            "third_early",
        )
        far1 = spread(ops1, cols_n, f1, "b", call)
        (f2,) = call(
            functools.partial(third, rows_n, first),
            [],
            [down, left, *basis, s1, a1, b1],
            [square],
            work,
            "third",
        )
        s1, a1, b1, a2, b2 = call(
            functools.partial(middle, rows_n, cols_n, first, ops0),
            [rhs, a_c, b_c],
            far0,
            [state] + [square] * 4,
            [pltpu.VMEM((n, n), full)] + [pltpu.VMEM((n, n), half)] * 3 + [pltpu.SemaphoreType.DMA((7,))],
            "middle",
        )
        (s2,) = call(
            functools.partial(middle_late, rows_n, cols_n, first, ops1),
            [],
            [s1, a1, b1, *far1],
            [state],
            [pltpu.VMEM((n, n), half)],
            "middle_late",
        )
        lasts = spread(ops2, cols_n, f2, "c", call)
        sent = [k for k, op in enumerate(ops2) if any(kind == "down" for _, _, kind, _ in op)]
        (s3,) = call(
            functools.partial(downs, cols_n, first, rows_n, [ops2[k] for k in sent]),
            [],
            [s2, a2, *[lasts[k] for k in sent]],
            [state],
            [pltpu.VMEM((n, n), half)],
            "downs",
        )
        return call(
            functools.partial(finish, rows_n, cols_n, first, ops2),
            [],
            [f0, f1, f2, s3, b2, *lasts],
            [square, state],
            [pltpu.VMEM((n, n), half), pltpu.VMEM((n, n), full), pltpu.VMEM((n, n), half), pltpu.SemaphoreType.DMA((4,))],
            "finish",
        )

    placed = (
        P("row", "col"),
        P(None, "row", "col"),
        P(None, "row", "col"),
        P("row", None),
        P("col", None),
        P("row"),
        P("col"),
    )
    return jax.shard_map(
        shards,
        mesh=mesh,
        in_specs=placed,
        out_specs=(P("row", "col"), P("row", "col")),
        check_vma=False,
    )
```

```python
import functools

import jax
import jax.numpy as jnp
from jax import lax
from jax.experimental import pallas as pl
from jax.experimental.pallas import tpu as pltpu
from jax.sharding import PartitionSpec as P


AXES = ("row", "col")
VMEM_SPEC = pl.BlockSpec(memory_space=pltpu.VMEM)
FAR_SPEC = pl.BlockSpec(memory_space=pltpu.HBM)


def plan(rows_n, cols_n, offset, gap, up_gap):
    rights, ups, last = [], [], []
    for i in range(rows_n):
        m = i + offset
        if 0 <= m < cols_n:
            targets = range(m + gap, cols_n)
            for chip in sorted({j // 2 for j in targets}, reverse=True):
                some = [(i, j) for j in targets if j // 2 == chip]
                (last if chip == m // 2 else rights).append(((i, m), some, "left"))
            ups += [((i, m), [(k, m)], "down") for k in range(i - up_gap + 1)]
    todo = rights + ups + last
    ops, forwards = [], []
    while todo:
        used_from, used_to, op = set(), set(), []
        waiting = {targets[0] for _, targets, kind in todo if kind == "down"}
        for item in list(todo):
            source, targets, kind = item
            for target in sorted(targets, key=lambda t: t in waiting):
                if source not in used_from and target not in used_to:
                    used_from.add(source)
                    used_to.add(target)
                    op.append((source, target, kind, None))
                    todo.remove(item)
                    forwards += [(target, other, kind, len(ops)) for other in targets if other != target]
                    break
        ops.append(op)
    return ops + [forwards] if forwards else ops


def one_of(me, ids):
    hit = me < 0
    for each in sorted(ids):
        hit = hit | (me == each)
    return hit


def place(cols_n):
    return lax.axis_index("row") * cols_n + lax.axis_index("col")


def level_of(rows_n):
    return rows_n - 1 - lax.axis_index("row") + lax.axis_index("col")


def dot(a, b):
    return lax.dot_general(a, b, (((1,), (0,)), ((), ())), preferred_element_type=jnp.float32)


def split(x):
    high = x.astype(jnp.bfloat16)
    return high, (x - high.astype(jnp.float32)).astype(jnp.bfloat16)


def put_left(ref, pair):
    n = pair[0].shape[1]
    ref[:, 0:n] = pair[0]
    ref[:, n : 2 * n] = pair[0]
    ref[:, 2 * n : 3 * n] = pair[1]


def put_right(ref, pair):
    n = pair[0].shape[0]
    ref[0:n] = pair[0]
    ref[n : 2 * n] = pair[1]
    ref[2 * n : 3 * n] = pair[0]


def dot_t(a, b):
    return lax.dot_general(a, b, (((1,), (1,)), ((), ())), preferred_element_type=jnp.float32)


def solve(state, uk, utk, vk, vl, inverse, lhs, mid):
    put_left(lhs, split(state))
    part = dot(lhs[...], vk[...])
    put_right(mid, split(part))
    part = dot(utk[...], mid[...]) * inverse[...]
    put_left(lhs, split(part))
    part = dot_t(lhs[...], vl[...])
    put_right(mid, split(part))
    return dot(uk[...], mid[...]).astype(jnp.bfloat16)


def put_lanes(ref, pair):
    n = pair[0].shape[1]
    ref[:, 0:n] = pair[0]
    ref[:, n : 2 * n] = pair[1]
    ref[:, 2 * n : 3 * n] = pair[0]


def set_inverse(inverse, av, bv):
    n = inverse.shape[0]
    alpha = jnp.transpose(jnp.broadcast_to(av[...][None, :], (128, n)))
    beta = bv[...][None, :]
    for c in range(0, n, 128):
        inverse[:, c : c + 128] = 1.0 / (alpha + beta[:, c : c + 128])


def set_right_basis(v, vk, vl):
    pair = split(v[...])
    put_right(vk, pair)
    put_lanes(vl, pair)


def set_left_basis(u, uk, utk):
    high, low = split(u[...])
    put_left(uk, (high, low))
    put_left(utk, (high.T, low.T))


def copies(pairs, sem):
    moves = [pltpu.make_async_copy(source, target, sem.at[n]) for n, (source, target) in enumerate(pairs)]
    for move in moves:
        move.start()
    return moves


def begin(rows_n, first, rhs, u_far, v_far, a_vals, b_vals, f0, s, u, v, av, bv, uk, utk, vk, vl, inverse, lhs, mid, sem):
    @pl.when(level_of(rows_n) == first)
    def _():
        moves = copies(((v_far, v), (rhs, s), (u_far, u), (a_vals, av), (b_vals, bv)), sem)
        moves[0].wait()
        set_right_basis(v, vk, vl)
        for move in moves[1:]:
            move.wait()
        set_left_basis(u, uk, utk)
        set_inverse(inverse, av, bv)
        f0[...] = solve(s[...], uk, utk, vk, vl, inverse, lhs, mid)


def prepare(rows_n, first, rhs, a_c, b_c, u_far, v_far, a_vals, b_vals, uk, utk, vk, vl, inverse, s, a0, b0, a1, b1, a2, b2, u, v, av, bv, sem):
    level = level_of(rows_n)
    terms = ((rhs, s), (a_c.at[0], a0), (b_c.at[0], b0), (a_c.at[1], a1), (b_c.at[1], b1))

    @pl.when((level > first) & (level <= first + 2))
    def _():
        moves = copies(((v_far, v), (u_far, u), (a_vals, av), (b_vals, bv), *terms), sem)
        moves[0].wait()
        set_right_basis(v, vk, vl)
        moves[1].wait()
        set_left_basis(u, uk, utk)
        moves[2].wait()
        moves[3].wait()
        set_inverse(inverse, av, bv)
        for move in moves[4:]:
            move.wait()

    @pl.when(level > first + 2)
    def _():
        for move in copies((*terms, (a_c.at[2], a2), (b_c.at[2], b2)), sem):
            move.wait()


def take_left(rows_n, level, left, s, coup_b, out):
    @pl.when(level_of(rows_n) == level)
    def _():
        out[...] = s[...] - dot(left[...], coup_b[...])


def second(rows_n, level, down, uk, utk, vk, vl, inverse, s, coup_a, f1, lhs, mid):
    @pl.when(level_of(rows_n) == level)
    def _():
        state = s[...] - dot(coup_a[...], down[...])
        f1[...] = solve(state, uk, utk, vk, vl, inverse, lhs, mid)


def third_early(rows_n, first, down, left, s, a0, b0, s1):
    @pl.when(level_of(rows_n) == first + 2)
    def _():
        s1[...] = s[...] - (dot(a0[...], down[...]) + dot(left[...], b0[...]))


def subtract(cols_n, ops, arrived, got, state, coup_a, coup_b, out, kinds=("down", "left")):
    out[...] = state[...]
    for kind in kinds:
        hits = pick(cols_n, ops, kind, arrived, got)

        @pl.when(hits)
        def _():
            out[...] -= dot(got[...], coup_b[...]) if kind == "left" else dot(coup_a[...], got[...])


def middle(rows_n, cols_n, first, ops, s1, a1, b1, *rest):
    arrived, (s2, got) = rest[: len(ops)], rest[len(ops) :]

    @pl.when(level_of(rows_n) > first + 2)
    def _():
        subtract(cols_n, ops, arrived, got, s1, a1, b1, s2)


def pick(cols_n, ops, kind, arrived, got):
    me = place(cols_n)
    any_hit = me < 0
    for op, ref in zip(ops, arrived):
        hit = one_of(me, [t[0] * cols_n + t[1] for _, t, k, _ in op if k == kind])
        any_hit = any_hit | hit

        @pl.when(hit)
        def _():
            got[...] = ref[...]

    return any_hit


def downs(cols_n, first, rows_n, ops, s2, a2, *rest):
    arrived, (s3, got) = rest[: len(ops)], rest[len(ops) :]

    @pl.when(level_of(rows_n) > first + 2)
    def _():
        subtract(cols_n, ops, arrived, got, s2, a2, None, s3, ("down",))


def finish(rows_n, cols_n, first, ops, f0, f1, f2, s3, b2, *rest):
    arrived, (out, nxt, got, mine, zeros, sem) = rest[: len(ops)], rest[len(ops) :]
    level = level_of(rows_n)
    n = s3.shape[0]
    step = n // 3
    active = level > first + 2
    for t, block in enumerate((f0, f1, f2)):

        @pl.when(level == first + t)
        def _():
            pltpu.make_async_copy(block, out, sem.at[3]).start()

    @pl.when((level < first) | active)
    def _():
        zeros[...] = jnp.zeros(zeros.shape, zeros.dtype)
        pltpu.make_async_copy(zeros, out, sem.at[3]).start()

    @pl.when(jnp.logical_not(active))
    def _():
        mine[...] = jnp.zeros(mine.shape, mine.dtype)
        for k in range(3):
            pltpu.make_async_copy(mine.at[pl.ds(k * step, step)], nxt.at[pl.ds(k * step, step)], sem.at[k]).start()

    @pl.when(active)
    def _():
        pick(cols_n, ops, "left", arrived, got)
        for k in range(3):
            rows = pl.ds(k * step, step)
            mine[rows] = s3[rows] - dot(got[rows], b2[...])
            pltpu.make_async_copy(mine.at[rows], nxt.at[rows], sem.at[k]).start()

    for k in range(3):
        pltpu.make_async_copy(mine.at[pl.ds(k * step, step)], nxt.at[pl.ds(k * step, step)], sem.at[k]).wait()
    pltpu.make_async_copy(zeros, out, sem.at[3]).wait()


def relay(cols_n, choices, own, *rest):
    *arrived, out = rest
    me = place(cols_n)
    hit = me < 0
    for ids, ref in zip(choices, arrived):
        mine = one_of(me, ids)
        hit = hit | mine

        @pl.when(mine)
        def _():
            out[...] = ref[...]

    @pl.when(jnp.logical_not(hit))
    def _():
        out[...] = own[...]


def spread(ops, cols_n, own, name, call):
    arrived = []
    for k, op in enumerate(ops):
        value = own
        earlier = sorted({f for *_, f in op if f is not None})
        if earlier:
            choices = [[s[0] * cols_n + s[1] for s, _, _, f in op if f == e] for e in earlier]
            (value,) = call(
                functools.partial(relay, cols_n, choices),
                [],
                [own, *[arrived[e] for e in earlier]],
                [jax.ShapeDtypeStruct(own.shape, own.dtype)],
                [],
                f"relay_{name}{k}",
            )
        pairs = [(s[0] * cols_n + s[1], t[0] * cols_n + t[1]) for s, t, _, _ in op]
        arrived.append(move(value, pairs))
    return arrived


def move(value, pairs):
    return lax.ppermute(value, AXES, pairs)


def solution(mesh):
    rows_n, cols_n = mesh.shape["row"], mesh.shape["col"]
    first = (rows_n + cols_n) // 2 - 2
    offset = first - rows_n + 1
    ops0 = plan(rows_n, cols_n, offset, 3, 3)
    ops1 = plan(rows_n, cols_n, offset + 1, 2, 2)
    ops2 = plan(rows_n, cols_n, offset + 2, 1, 1)

    def owners(t):
        return [(i, i + offset + t) for i in range(rows_n) if 0 <= i + offset + t < cols_n]

    def up(t, far):
        return [(i * cols_n + j, (i - far) * cols_n + j) for i, j in owners(t) if i >= far]

    def right(t, far):
        return [(i * cols_n + j, i * cols_n + j + far) for i, j in owners(t) if j + far < cols_n]

    def shards(rhs, a_c, b_c, u, v, a_vals, b_vals):
        n = rhs.shape[0]
        half, full = jnp.bfloat16, jnp.float32
        square = jax.ShapeDtypeStruct((n, n), half)
        wide, tall = jax.ShapeDtypeStruct((n, 3 * n), half), jax.ShapeDtypeStruct((3 * n, n), half)
        state = jax.ShapeDtypeStruct((n, n), full)
        loads = [pltpu.VMEM((n, n), full)] * 3 + [pltpu.VMEM((n,), full)] * 2
        basis_work = [pltpu.VMEM((n, 3 * n), half)] * 2 + [pltpu.VMEM((3 * n, n), half), pltpu.VMEM((n, 3 * n), half), pltpu.VMEM((n, n), full)]
        work = [pltpu.VMEM((n, 3 * n), half), pltpu.VMEM((3 * n, n), half)]

        def call(kernel, far, near, outs, scratch, name):
            ins = [pltpu.with_memory_space_constraint(x, pltpu.HBM) for x in far] + list(near)
            return pl.pallas_call(
                kernel,
                out_shape=outs,
                in_specs=[FAR_SPEC] * len(far) + [VMEM_SPEC] * len(near),
                out_specs=[FAR_SPEC if name == "finish" else VMEM_SPEC] * len(outs),
                scratch_shapes=scratch,
                compiler_params=pltpu.CompilerParams(vmem_limit_bytes=24 << 20),
            )(*ins)

        basis_shapes = [wide, wide, tall, wide, state]
        (f0,) = call(
            functools.partial(begin, rows_n, first),
            [rhs, u, v, a_vals, b_vals],
            [],
            [square],
            loads + basis_work + work + [pltpu.SemaphoreType.DMA((5,))],
            "begin",
        )

        def advance(t, down, left, state_in, coup_a, coup_b):
            (part,) = call(
                functools.partial(take_left, rows_n, first + t + 1),
                [],
                [left, state_in, coup_b],
                [state],
                [],
                f"left{t}",
            )
            return call(
                functools.partial(second, rows_n, first + t + 1),
                [],
                [down, *basis, part, coup_a],
                [square],
                work,
                f"solve{t}",
            )

        down = move(f0, up(0, 1))
        left = move(f0, right(0, 1))
        down_far = move(f0, up(0, 2))
        left_far = move(f0, right(0, 2))
        far0 = spread(ops0, cols_n, f0, "a", call)
        *basis, s, a0, b0, a1, b1, a2, b2 = call(
            functools.partial(prepare, rows_n, first),
            [rhs, a_c, b_c, u, v, a_vals, b_vals],
            [],
            basis_shapes + [state] + [square] * 6,
            loads[1:] + [pltpu.SemaphoreType.DMA((9,))],
            "prepare",
        )
        (f1,) = advance(0, down, left, s, a0, b0)
        down = move(f1, up(1, 1))
        left = move(f1, right(1, 1))
        (s1,) = call(
            functools.partial(third_early, rows_n, first),
            [],
            [down_far, left_far, s, a0, b0],
            [state],
            [],
            "third_early",
        )
        far1 = spread(ops1, cols_n, f1, "b", call)
        (f2,) = advance(1, down, left, s1, a1, b1)
        for k, (ops, far, a, b) in enumerate(((ops0, far0, a0, b0), (ops1, far1, a1, b1))):
            (s,) = call(
                functools.partial(middle, rows_n, cols_n, first, ops),
                [],
                [s, a, b, *far],
                [state],
                [pltpu.VMEM((n, n), half)],
                f"middle{k}",
            )
        lasts = spread(ops2, cols_n, f2, "c", call)
        sent = [k for k, op in enumerate(ops2) if any(kind == "down" for _, _, kind, _ in op)]
        (s3,) = call(
            functools.partial(downs, cols_n, first, rows_n, [ops2[k] for k in sent]),
            [],
            [s, a2, *[lasts[k] for k in sent]],
            [state],
            [pltpu.VMEM((n, n), half)],
            "downs",
        )
        return call(
            functools.partial(finish, rows_n, cols_n, first, ops2),
            [],
            [f0, f1, f2, s3, b2, *lasts],
            [square, state],
            [pltpu.VMEM((n, n), half), pltpu.VMEM((n, n), full), pltpu.VMEM((n, n), half), pltpu.SemaphoreType.DMA((4,))],
            "finish",
        )

    placed = (
        P("row", "col"),
        P(None, "row", "col"),
        P(None, "row", "col"),
        P("row", None),
        P("col", None),
        P("row"),
        P("col"),
    )
    return jax.shard_map(
        shards,
        mesh=mesh,
        in_specs=placed,
        out_specs=(P("row", "col"), P("row", "col")),
        check_vma=False,
    )
```

```python
import functools

import jax
import jax.numpy as jnp
from jax import lax
from jax.experimental import pallas as pl
from jax.experimental.pallas import tpu as pltpu
from jax.sharding import PartitionSpec as P


AXES = ("row", "col")
VMEM_SPEC = pl.BlockSpec(memory_space=pltpu.VMEM)
FAR_SPEC = pl.BlockSpec(memory_space=pltpu.HBM)


def plan(rows_n, cols_n, offset, gap, up_gap):
    rights, ups, last = [], [], []
    for i in range(rows_n):
        m = i + offset
        if 0 <= m < cols_n:
            targets = range(m + gap, cols_n)
            for chip in sorted({j // 2 for j in targets}, reverse=True):
                some = [(i, j) for j in targets if j // 2 == chip]
                (last if chip == m // 2 else rights).append(((i, m), some, "left"))
            ups += [((i, m), [(k, m)], "down") for k in range(i - up_gap + 1)]
    todo = rights + ups + last
    ops, forwards = [], []
    while todo:
        used_from, used_to, op = set(), set(), []
        busy = [source for source, _, _ in todo]
        waiting = {targets[0]: busy.count(source) for source, targets, kind in todo if kind == "down"}
        for item in list(todo):
            source, targets, kind = item
            for target in sorted(targets, key=lambda t: (waiting.get(t, 0), -t[1])):
                if source not in used_from and target not in used_to:
                    used_from.add(source)
                    used_to.add(target)
                    op.append((source, target, kind, None))
                    todo.remove(item)
                    forwards += [(target, other, kind, len(ops)) for other in targets if other != target]
                    break
        ops.append(op)
    return ops + [forwards] if forwards else ops


def with_near(ops, near):
    far = {source[0]: target[1] // 2 != source[1] // 2 for source, target in near}
    mixed = [[], []]
    for source, target in near:
        mixed[0 if far[source[0]] else 1].append((source, target, "near", None))
    for edge in ops[0]:
        mixed[1 if far.get(edge[0][0], False) else 0].append(edge)
    ops = mixed + ops[1:]
    came = {target: k for k, op in enumerate(ops) for _, target, kind, handed in op if kind == "left" and handed is None}
    return [[edge if edge[3] is None else (*edge[:3], came[edge[0]]) for edge in op] for op in ops]


def one_of(me, ids):
    hit = me < 0
    for each in sorted(ids):
        hit = hit | (me == each)
    return hit


def place(cols_n):
    return lax.axis_index("row") * cols_n + lax.axis_index("col")


def level_of(rows_n):
    return rows_n - 1 - lax.axis_index("row") + lax.axis_index("col")


def dot(a, b):
    return lax.dot_general(a, b, (((1,), (0,)), ((), ())), preferred_element_type=jnp.float32)


def split(x):
    high = x.astype(jnp.bfloat16)
    return high, (x - high.astype(jnp.float32)).astype(jnp.bfloat16)


def put_left(ref, pair):
    n = pair[0].shape[1]
    ref[:, 0:n] = pair[0]
    ref[:, n : 2 * n] = pair[0]
    ref[:, 2 * n : 3 * n] = pair[1]


def put_right(ref, pair):
    n = pair[0].shape[0]
    ref[0:n] = pair[0]
    ref[n : 2 * n] = pair[1]
    ref[2 * n : 3 * n] = pair[0]


def dot_t(a, b):
    return lax.dot_general(a, b, (((1,), (1,)), ((), ())), preferred_element_type=jnp.float32)


def spectral(state, utk, vk, lhs, mid):
    put_left(lhs, split(state))
    part = dot(lhs[...], vk[...])
    put_right(mid, split(part))
    return dot(utk[...], mid[...])


def back(part, uk, vl, lhs, mid):
    put_left(lhs, split(part))
    part = dot_t(lhs[...], vl[...])
    put_right(mid, split(part))
    return dot(uk[...], mid[...]).astype(jnp.bfloat16)


def put_lanes(ref, pair):
    n = pair[0].shape[1]
    ref[:, 0:n] = pair[0]
    ref[:, n : 2 * n] = pair[1]
    ref[:, 2 * n : 3 * n] = pair[0]


def set_inverse(inverse, av, bv):
    n = inverse.shape[0]
    alpha = jnp.transpose(jnp.broadcast_to(av[...][None, :], (128, n)))
    beta = bv[...][None, :]
    for c in range(0, n, 128):
        inverse[:, c : c + 128] = 1.0 / (alpha + beta[:, c : c + 128])


def set_right_basis(v, vk, vl):
    pair = split(v[...])
    put_right(vk, pair)
    put_lanes(vl, pair)


def set_left_basis(u, uk, utk):
    high, low = split(u[...])
    put_left(uk, (high, low))
    put_left(utk, (high.T, low.T))


def copies(pairs, sem):
    moves = [pltpu.make_async_copy(source, target, sem.at[n]) for n, (source, target) in enumerate(pairs)]
    for move in moves:
        move.start()
    return moves


def begin(rows_n, first, rhs, u_far, v_far, a_vals, b_vals, f0, s, u, v, av, bv, uk, utk, vk, vl, inverse, lhs, mid, sem):
    @pl.when(level_of(rows_n) == first)
    def _():
        moves = copies(((v_far, v), (rhs, s), (u_far, u), (a_vals, av), (b_vals, bv)), sem)
        moves[0].wait()
        set_right_basis(v, vk, vl)
        for move in moves[1:]:
            move.wait()
        set_left_basis(u, uk, utk)
        set_inverse(inverse, av, bv)
        part = spectral(s[...], utk, vk, lhs, mid) * inverse[...]
        f0[...] = back(part, uk, vl, lhs, mid)


def prepare(rows_n, first, rhs, a_c, b_c, u_far, v_far, a_vals, b_vals, uk, utk, vk, vl, inverse, coup, s, a0, b0, a1, b1, a2, b2, u, v, av, bv, both, sem):
    level = level_of(rows_n)
    terms = ((rhs, s), (a_c.at[0], a0), (b_c.at[0], b0), (a_c.at[1], a1), (b_c.at[1], b1))

    @pl.when((level > first) & (level <= first + 2))
    def _():
        moves = copies(((v_far, v), (u_far, u), (a_vals, av), (b_vals, bv), *terms), sem)
        moves[0].wait()
        set_right_basis(v, vk, vl)
        moves[1].wait()
        set_left_basis(u, uk, utk)
        moves[2].wait()
        moves[3].wait()
        set_inverse(inverse, av, bv)
        for move in moves[4:]:
            move.wait()
        n = u.shape[0]
        for t, a in enumerate((a0, a1)):

            @pl.when(level == first + 1 + t)
            def _():
                both[0:n] = a[...]
                both[n:] = a[...]

        put_left(coup, split(dot(utk[:, n:], both[...])))

    @pl.when(level > first + 2)
    def _():
        for move in copies((*terms, (a_c.at[2], a2), (b_c.at[2], b2)), sem):
            move.wait()


def take_left(rows_n, level, near, far, s, coup_b, utk, vk, out, lhs, mid):
    even = lax.rem(lax.axis_index("col"), 2) == 0

    @pl.when(level_of(rows_n) == level)
    def _():
        left = jnp.where(even, far[...], near[...])
        out[...] = spectral(s[...] - dot(left, coup_b[...]), utk, vk, lhs, mid)


def finish_solve(rows_n, level, down, y, coup, uk, vk, vl, inverse, f, lhs, mid):
    @pl.when(level_of(rows_n) == level)
    def _():
        n = y.shape[0]
        lhs[:, 0:n] = down[...]
        lhs[:, n : 2 * n] = down[...]
        part = dot(lhs[:, 0 : 2 * n], vk[0 : 2 * n])
        put_right(mid, split(part))
        part = (y[...] - dot(coup[...], mid[...])) * inverse[...]
        f[...] = back(part, uk, vl, lhs, mid)


def third_early(rows_n, first, down, left, s, a0, b0, s1):
    @pl.when(level_of(rows_n) == first + 2)
    def _():
        s1[...] = s[...] - (dot(a0[...], down[...]) + dot(left[...], b0[...]))


def subtract(cols_n, ops, arrived, got, state, coup_a, coup_b, out, kinds=("down", "left")):
    out[...] = state[...]
    for kind in kinds:
        hits = pick(cols_n, ops, kind, arrived, got)

        @pl.when(hits)
        def _():
            out[...] -= dot(got[...], coup_b[...]) if kind == "left" else dot(coup_a[...], got[...])


def middle(rows_n, cols_n, first, ops, s1, a1, b1, *rest):
    arrived, (s2, got) = rest[: len(ops)], rest[len(ops) :]

    @pl.when(level_of(rows_n) > first + 2)
    def _():
        subtract(cols_n, ops, arrived, got, s1, a1, b1, s2)


def pick(cols_n, ops, kind, arrived, got):
    me = place(cols_n)
    any_hit = me < 0
    for op, ref in zip(ops, arrived):
        hit = one_of(me, [t[0] * cols_n + t[1] for _, t, k, _ in op if k == kind])
        any_hit = any_hit | hit

        @pl.when(hit)
        def _():
            got[...] = ref[...]

    return any_hit


def downs(cols_n, first, rows_n, ops, s2, a2, *rest):
    arrived, (s3, got) = rest[: len(ops)], rest[len(ops) :]

    @pl.when(level_of(rows_n) > first + 2)
    def _():
        subtract(cols_n, ops, arrived, got, s2, a2, None, s3, ("down",))


def publish(rows_n, first, f0, f1, f2, out, zeros, sem):
    level = level_of(rows_n)
    for t, block in enumerate((f0, f1, f2)):

        @pl.when(level == first + t)
        def _():
            pltpu.make_async_copy(block, out, sem).start()

    @pl.when((level < first) | (level > first + 2))
    def _():
        zeros[...] = jnp.zeros(zeros.shape, zeros.dtype)
        pltpu.make_async_copy(zeros, out, sem).start()

    pltpu.make_async_copy(zeros, out, sem).wait()


def finish(rows_n, cols_n, first, ops, s3, b2, *rest):
    arrived, (nxt, got, mine, sem) = rest[: len(ops)], rest[len(ops) :]
    n = s3.shape[0]
    step = n // 3
    active = level_of(rows_n) > first + 2

    @pl.when(jnp.logical_not(active))
    def _():
        mine[...] = jnp.zeros(mine.shape, mine.dtype)
        for k in range(3):
            pltpu.make_async_copy(mine.at[pl.ds(k * step, step)], nxt.at[pl.ds(k * step, step)], sem.at[k]).start()

    @pl.when(active)
    def _():
        pick(cols_n, ops, "left", arrived, got)
        for k in range(3):
            rows = pl.ds(k * step, step)
            mine[rows] = s3[rows] - dot(got[rows], b2[...])
            pltpu.make_async_copy(mine.at[rows], nxt.at[rows], sem.at[k]).start()

    for k in range(3):
        pltpu.make_async_copy(mine.at[pl.ds(k * step, step)], nxt.at[pl.ds(k * step, step)], sem.at[k]).wait()


def relay(cols_n, choices, own, *rest):
    *arrived, out = rest
    me = place(cols_n)
    hit = me < 0
    for ids, ref in zip(choices, arrived):
        mine = one_of(me, ids)
        hit = hit | mine

        @pl.when(mine)
        def _():
            out[...] = ref[...]

    @pl.when(jnp.logical_not(hit))
    def _():
        out[...] = own[...]


def spread(ops, cols_n, own, name, call):
    arrived = []
    for k, op in enumerate(ops):
        value = own
        earlier = sorted({f for *_, f in op if f is not None})
        if earlier:
            choices = [[s[0] * cols_n + s[1] for s, _, _, f in op if f == e] for e in earlier]
            (value,) = call(
                functools.partial(relay, cols_n, choices),
                [],
                [own, *[arrived[e] for e in earlier]],
                [jax.ShapeDtypeStruct(own.shape, own.dtype)],
                [],
                f"relay_{name}{k}",
            )
        pairs = [(s[0] * cols_n + s[1], t[0] * cols_n + t[1]) for s, t, _, _ in op]
        arrived.append(move(value, pairs))
    return arrived


def move(value, pairs):
    return lax.ppermute(value, AXES, pairs)


def solution(mesh):
    rows_n, cols_n = mesh.shape["row"], mesh.shape["col"]
    first = (rows_n + cols_n) // 2 - 2
    offset = first - rows_n + 1
    ops0 = plan(rows_n, cols_n, offset, 3, 3)
    ops2 = plan(rows_n, cols_n, offset + 2, 1, 1)

    def owners(t):
        return [(i, i + offset + t) for i in range(rows_n) if 0 <= i + offset + t < cols_n]

    near = [((i, j), (i, j + 1)) for i, j in owners(1) if j + 1 < cols_n]
    ops1 = with_near(plan(rows_n, cols_n, offset + 1, 2, 2), near)

    def up(t, far):
        return [(i * cols_n + j, (i - far) * cols_n + j) for i, j in owners(t) if i >= far]

    def right(t, far):
        return [(i * cols_n + j, i * cols_n + j + far) for i, j in owners(t) if j + far < cols_n]

    def shards(rhs, a_c, b_c, u, v, a_vals, b_vals):
        n = rhs.shape[0]
        half, full = jnp.bfloat16, jnp.float32
        square = jax.ShapeDtypeStruct((n, n), half)
        wide, tall = jax.ShapeDtypeStruct((n, 3 * n), half), jax.ShapeDtypeStruct((3 * n, n), half)
        state = jax.ShapeDtypeStruct((n, n), full)
        loads = [pltpu.VMEM((n, n), full)] * 3 + [pltpu.VMEM((n,), full)] * 2
        basis_work = [pltpu.VMEM((n, 3 * n), half)] * 2 + [pltpu.VMEM((3 * n, n), half), pltpu.VMEM((n, 3 * n), half), pltpu.VMEM((n, n), full)]
        work = [pltpu.VMEM((n, 3 * n), half), pltpu.VMEM((3 * n, n), half)]

        def call(kernel, far, near, outs, scratch, name):
            ins = [pltpu.with_memory_space_constraint(x, pltpu.HBM) for x in far] + list(near)
            return pl.pallas_call(
                kernel,
                out_shape=outs,
                in_specs=[FAR_SPEC] * len(far) + [VMEM_SPEC] * len(near),
                out_specs=[FAR_SPEC if name in ("finish", "publish") else VMEM_SPEC] * len(outs),
                scratch_shapes=scratch,
                compiler_params=pltpu.CompilerParams(vmem_limit_bytes=24 << 20),
            )(*ins)

        basis_shapes = [wide, wide, tall, wide, state]
        (f0,) = call(
            functools.partial(begin, rows_n, first),
            [rhs, u, v, a_vals, b_vals],
            [],
            [square],
            loads + basis_work + work + [pltpu.SemaphoreType.DMA((5,))],
            "begin",
        )

        def advance(t, down, near, far, state_in, coup_b):
            uk, utk, vk, vl, inverse = basis
            (y,) = call(
                functools.partial(take_left, rows_n, first + t + 1),
                [],
                [near, far, state_in, coup_b, utk, vk],
                [state],
                work,
                f"left{t}",
            )
            return call(
                functools.partial(finish_solve, rows_n, first + t + 1),
                [],
                [down, y, coup, uk, vk, vl, inverse],
                [square],
                work,
                f"solve{t}",
            )

        down = move(f0, up(0, 1))
        left = move(f0, right(0, 1))
        down_far = move(f0, up(0, 2))
        left_far = move(f0, right(0, 2))
        far0 = spread(ops0, cols_n, f0, "a", call)
        *basis, coup, s, a0, b0, a1, b1, a2, b2 = call(
            functools.partial(prepare, rows_n, first),
            [rhs, a_c, b_c, u, v, a_vals, b_vals],
            [],
            basis_shapes + [wide, state] + [square] * 6,
            loads[1:] + [pltpu.VMEM((2 * n, n), half), pltpu.SemaphoreType.DMA((9,))],
            "prepare",
        )
        (f1,) = advance(0, down, left, left, s, b0)
        down = move(f1, up(1, 1))
        (s1,) = call(
            functools.partial(third_early, rows_n, first),
            [],
            [down_far, left_far, s, a0, b0],
            [state],
            [],
            "third_early",
        )
        far1 = spread(ops1, cols_n, f1, "b", call)
        (f2,) = advance(1, down, far1[1], far1[0], s1, b1)
        for k, (ops, far, a, b) in enumerate(((ops0, far0, a0, b0), (ops1, far1, a1, b1))):
            (s,) = call(
                functools.partial(middle, rows_n, cols_n, first, ops),
                [],
                [s, a, b, *far],
                [state],
                [pltpu.VMEM((n, n), half)],
                f"middle{k}",
            )
        lasts = spread(ops2, cols_n, f2, "c", call)
        sent = [k for k, op in enumerate(ops2) if any(kind == "down" for _, _, kind, _ in op)]
        (s3,) = call(
            functools.partial(downs, cols_n, first, rows_n, [ops2[k] for k in sent]),
            [],
            [s, a2, *[lasts[k] for k in sent]],
            [state],
            [pltpu.VMEM((n, n), half)],
            "downs",
        )
        (out,) = call(
            functools.partial(publish, rows_n, first),
            [],
            [f0, f1, f2],
            [square],
            [pltpu.VMEM((n, n), half), pltpu.SemaphoreType.DMA],
            "publish",
        )
        (nxt,) = call(
            functools.partial(finish, rows_n, cols_n, first, ops2),
            [],
            [s3, b2, *lasts],
            [state],
            [pltpu.VMEM((n, n), half), pltpu.VMEM((n, n), full), pltpu.SemaphoreType.DMA((3,))],
            "finish",
        )
        return out, nxt

    placed = (
        P("row", "col"),
        P(None, "row", "col"),
        P(None, "row", "col"),
        P("row", None),
        P("col", None),
        P("row"),
        P("col"),
    )
    return jax.shard_map(
        shards,
        mesh=mesh,
        in_specs=placed,
        out_specs=(P("row", "col"), P("row", "col")),
        check_vma=False,
    )
```

```python
import functools

import jax
import jax.numpy as jnp
from jax import lax
from jax.experimental import pallas as pl
from jax.experimental.pallas import tpu as pltpu
from jax.sharding import PartitionSpec as P


AXES = ("row", "col")
VMEM_SPEC = pl.BlockSpec(memory_space=pltpu.VMEM)
FAR_SPEC = pl.BlockSpec(memory_space=pltpu.HBM)


def plan(rows_n, cols_n, offset, gap, up_gap):
    rights, ups, last = [], [], []
    for i in range(rows_n):
        m = i + offset
        if 0 <= m < cols_n:
            targets = range(m + gap, cols_n)
            for chip in sorted({j // 2 for j in targets}, reverse=True):
                some = [(i, j) for j in targets if j // 2 == chip]
                (last if chip == m // 2 else rights).append(((i, m), some, "left"))
            ups += [((i, m), [(k, m)], "down") for k in range(i - up_gap + 1)]
    todo = rights + ups + last
    ops, forwards = [], []
    while todo:
        used_from, used_to, op = set(), set(), []
        busy = [source for source, _, _ in todo]
        waiting = {targets[0]: busy.count(source) for source, targets, kind in todo if kind == "down"}
        for item in list(todo):
            source, targets, kind = item
            for target in sorted(targets, key=lambda t: (waiting.get(t, 0), -t[1])):
                if source not in used_from and target not in used_to:
                    used_from.add(source)
                    used_to.add(target)
                    op.append((source, target, kind, None))
                    todo.remove(item)
                    forwards += [(target, other, kind, len(ops)) for other in targets if other != target]
                    break
        ops.append(op)
    return ops + [forwards] if forwards else ops


def one_of(me, ids):
    hit = me < 0
    for each in sorted(ids):
        hit = hit | (me == each)
    return hit


def place(cols_n):
    return lax.axis_index("row") * cols_n + lax.axis_index("col")


def level_of(rows_n):
    return rows_n - 1 - lax.axis_index("row") + lax.axis_index("col")


def dot(a, b):
    return lax.dot_general(a, b, (((1,), (0,)), ((), ())), preferred_element_type=jnp.float32)


def split(x):
    high = x.astype(jnp.bfloat16)
    return high, (x - high.astype(jnp.float32)).astype(jnp.bfloat16)


def put_left(ref, pair):
    n = pair[0].shape[1]
    ref[:, 0:n] = pair[0]
    ref[:, n : 2 * n] = pair[0]
    ref[:, 2 * n : 3 * n] = pair[1]


def put_right(ref, pair):
    n = pair[0].shape[0]
    ref[0:n] = pair[0]
    ref[n : 2 * n] = pair[1]
    ref[2 * n : 3 * n] = pair[0]


def dot_t(a, b):
    return lax.dot_general(a, b, (((1,), (1,)), ((), ())), preferred_element_type=jnp.float32)


def spectral(state, utk, vk, lhs, mid):
    put_left(lhs, split(state))
    part = dot(lhs[...], vk[...])
    put_right(mid, split(part))
    return dot(utk[...], mid[...])


def back(part, uk, vl, lhs, mid):
    put_left(lhs, split(part))
    part = dot_t(lhs[...], vl[...])
    put_right(mid, split(part))
    return dot(uk[...], mid[...]).astype(jnp.bfloat16)


def put_lanes(ref, pair):
    n = pair[0].shape[1]
    ref[:, 0:n] = pair[0]
    ref[:, n : 2 * n] = pair[1]
    ref[:, 2 * n : 3 * n] = pair[0]


def set_inverse(inverse, av, bv):
    n = inverse.shape[0]
    alpha = jnp.transpose(jnp.broadcast_to(av[...][None, :], (128, n)))
    beta = bv[...][None, :]
    for c in range(0, n, 128):
        inverse[:, c : c + 128] = 1.0 / (alpha + beta[:, c : c + 128])


def set_right_basis(v, vk, vl):
    pair = split(v[...])
    put_right(vk, pair)
    put_lanes(vl, pair)


def set_left_basis(u, uk, utk):
    high, low = split(u[...])
    put_left(uk, (high, low))
    put_left(utk, (high.T, low.T))


def copies(pairs, sem):
    moves = [pltpu.make_async_copy(source, target, sem.at[n]) for n, (source, target) in enumerate(pairs)]
    for move in moves:
        move.start()
    return moves


def begin(rows_n, first, rhs, u_far, v_far, a_vals, b_vals, f0, s, u, v, av, bv, uk, utk, vk, vl, inverse, lhs, mid, sem):
    @pl.when(level_of(rows_n) == first)
    def _():
        moves = copies(((v_far, v), (rhs, s), (u_far, u), (a_vals, av), (b_vals, bv)), sem)
        moves[0].wait()
        set_right_basis(v, vk, vl)
        for move in moves[1:]:
            move.wait()
        set_left_basis(u, uk, utk)
        set_inverse(inverse, av, bv)
        part = spectral(s[...], utk, vk, lhs, mid) * inverse[...]
        f0[...] = back(part, uk, vl, lhs, mid)


def prepare(rows_n, first, rhs, a_c, b_c, u_far, v_far, a_vals, b_vals, uk, utk, vk, vl, inverse, coup, s, a0, b0, a1, b1, a2, b2, u, v, av, bv, both, sem):
    level = level_of(rows_n)
    terms = ((rhs, s), (a_c.at[0], a0), (b_c.at[0], b0), (a_c.at[1], a1), (b_c.at[1], b1))

    @pl.when((level > first) & (level <= first + 2))
    def _():
        moves = copies(((v_far, v), (u_far, u), (a_vals, av), (b_vals, bv), *terms), sem)
        moves[0].wait()
        set_right_basis(v, vk, vl)
        moves[1].wait()
        set_left_basis(u, uk, utk)
        moves[2].wait()
        moves[3].wait()
        set_inverse(inverse, av, bv)
        for move in moves[4:]:
            move.wait()
        n = u.shape[0]
        for t, a in enumerate((a0, a1)):

            @pl.when(level == first + 1 + t)
            def _():
                both[0:n] = a[...]
                both[n:] = a[...]

        put_left(coup, split(dot(utk[:, n:], both[...])))

    @pl.when(level > first + 2)
    def _():
        for move in copies((*terms, (a_c.at[2], a2), (b_c.at[2], b2)), sem):
            move.wait()


def take_left(rows_n, level, left, s, coup_b, utk, vk, out, lhs, mid):
    @pl.when(level_of(rows_n) == level)
    def _():
        out[...] = spectral(s[...] - dot(left[...], coup_b[...]), utk, vk, lhs, mid)


def finish_solve(rows_n, level, down, y, coup, uk, vk, vl, inverse, f, lhs, mid):
    @pl.when(level_of(rows_n) == level)
    def _():
        n = y.shape[0]
        lhs[:, 0:n] = down[...]
        lhs[:, n : 2 * n] = down[...]
        part = dot(lhs[:, 0 : 2 * n], vk[0 : 2 * n])
        put_right(mid, split(part))
        part = (y[...] - dot(coup[...], mid[...])) * inverse[...]
        f[...] = back(part, uk, vl, lhs, mid)


def third_early(rows_n, first, down, left, s, a0, b0, s1):
    @pl.when(level_of(rows_n) == first + 2)
    def _():
        s1[...] = s[...] - (dot(a0[...], down[...]) + dot(left[...], b0[...]))


def subtract(cols_n, ops, arrived, got, state, coup_a, coup_b, out, kinds=("down", "left")):
    out[...] = state[...]
    for kind in kinds:
        hits = pick(cols_n, ops, kind, arrived, got)

        @pl.when(hits)
        def _():
            out[...] -= dot(got[...], coup_b[...]) if kind == "left" else dot(coup_a[...], got[...])


def middle(rows_n, cols_n, first, ops, s1, a1, b1, *rest):
    arrived, (s2, got) = rest[: len(ops)], rest[len(ops) :]

    @pl.when(level_of(rows_n) > first + 2)
    def _():
        subtract(cols_n, ops, arrived, got, s1, a1, b1, s2)


def pick(cols_n, ops, kind, arrived, got):
    me = place(cols_n)
    any_hit = me < 0
    for op, ref in zip(ops, arrived):
        hit = one_of(me, [t[0] * cols_n + t[1] for _, t, k, _ in op if k == kind])
        any_hit = any_hit | hit

        @pl.when(hit)
        def _():
            got[...] = ref[...]

    return any_hit


def downs(cols_n, first, rows_n, ops, s2, a2, *rest):
    arrived, (s3, got) = rest[: len(ops)], rest[len(ops) :]

    @pl.when(level_of(rows_n) > first + 2)
    def _():
        subtract(cols_n, ops, arrived, got, s2, a2, None, s3, ("down",))


def publish(rows_n, first, f0, f1, f2, out, zeros, sem):
    level = level_of(rows_n)
    for t, block in enumerate((f0, f1, f2)):

        @pl.when(level == first + t)
        def _():
            pltpu.make_async_copy(block, out, sem).start()

    @pl.when((level < first) | (level > first + 2))
    def _():
        zeros[...] = jnp.zeros(zeros.shape, zeros.dtype)
        pltpu.make_async_copy(zeros, out, sem).start()

    pltpu.make_async_copy(zeros, out, sem).wait()


def finish(rows_n, cols_n, first, ops, s3, b2, *rest):
    arrived, (nxt, got, mine, sem) = rest[: len(ops)], rest[len(ops) :]
    n = s3.shape[0]
    step = n // 3
    active = level_of(rows_n) > first + 2

    @pl.when(jnp.logical_not(active))
    def _():
        mine[...] = jnp.zeros(mine.shape, mine.dtype)
        for k in range(3):
            pltpu.make_async_copy(mine.at[pl.ds(k * step, step)], nxt.at[pl.ds(k * step, step)], sem.at[k]).start()

    @pl.when(active)
    def _():
        pick(cols_n, ops, "left", arrived, got)
        for k in range(3):
            rows = pl.ds(k * step, step)
            mine[rows] = s3[rows] - dot(got[rows], b2[...])
            pltpu.make_async_copy(mine.at[rows], nxt.at[rows], sem.at[k]).start()

    for k in range(3):
        pltpu.make_async_copy(mine.at[pl.ds(k * step, step)], nxt.at[pl.ds(k * step, step)], sem.at[k]).wait()


def relay(cols_n, choices, own, *rest):
    *arrived, out = rest
    me = place(cols_n)
    hit = me < 0
    for ids, ref in zip(choices, arrived):
        mine = one_of(me, ids)
        hit = hit | mine

        @pl.when(mine)
        def _():
            out[...] = ref[...]

    @pl.when(jnp.logical_not(hit))
    def _():
        out[...] = own[...]


def spread(ops, cols_n, own, name, call):
    arrived = []
    for k, op in enumerate(ops):
        value = own
        earlier = sorted({f for *_, f in op if f is not None})
        if earlier:
            choices = [[s[0] * cols_n + s[1] for s, _, _, f in op if f == e] for e in earlier]
            (value,) = call(
                functools.partial(relay, cols_n, choices),
                [],
                [own, *[arrived[e] for e in earlier]],
                [jax.ShapeDtypeStruct(own.shape, own.dtype)],
                [],
                f"relay_{name}{k}",
            )
        pairs = [(s[0] * cols_n + s[1], t[0] * cols_n + t[1]) for s, t, _, _ in op]
        arrived.append(move(value, pairs))
    return arrived


def move(value, pairs):
    return lax.ppermute(value, AXES, pairs)


def solution(mesh):
    rows_n, cols_n = mesh.shape["row"], mesh.shape["col"]
    first = (rows_n + cols_n) // 2 - 2
    offset = first - rows_n + 1
    ops0 = plan(rows_n, cols_n, offset, 3, 3)
    ops1 = plan(rows_n, cols_n, offset + 1, 2, 2)
    ops2 = plan(rows_n, cols_n, offset + 2, 1, 1)

    def owners(t):
        return [(i, i + offset + t) for i in range(rows_n) if 0 <= i + offset + t < cols_n]

    def up(t, far):
        return [(i * cols_n + j, (i - far) * cols_n + j) for i, j in owners(t) if i >= far]

    def right(t, far):
        return [(i * cols_n + j, i * cols_n + j + far) for i, j in owners(t) if j + far < cols_n]

    def shards(rhs, a_c, b_c, u, v, a_vals, b_vals):
        n = rhs.shape[0]
        half, full = jnp.bfloat16, jnp.float32
        square = jax.ShapeDtypeStruct((n, n), half)
        wide, tall = jax.ShapeDtypeStruct((n, 3 * n), half), jax.ShapeDtypeStruct((3 * n, n), half)
        state = jax.ShapeDtypeStruct((n, n), full)
        loads = [pltpu.VMEM((n, n), full)] * 3 + [pltpu.VMEM((n,), full)] * 2
        basis_work = [pltpu.VMEM((n, 3 * n), half)] * 2 + [pltpu.VMEM((3 * n, n), half), pltpu.VMEM((n, 3 * n), half), pltpu.VMEM((n, n), full)]
        work = [pltpu.VMEM((n, 3 * n), half), pltpu.VMEM((3 * n, n), half)]

        def call(kernel, far, near, outs, scratch, name):
            ins = [pltpu.with_memory_space_constraint(x, pltpu.HBM) for x in far] + list(near)
            return pl.pallas_call(
                kernel,
                out_shape=outs,
                in_specs=[FAR_SPEC] * len(far) + [VMEM_SPEC] * len(near),
                out_specs=[FAR_SPEC if name in ("finish", "publish") else VMEM_SPEC] * len(outs),
                scratch_shapes=scratch,
                compiler_params=pltpu.CompilerParams(vmem_limit_bytes=24 << 20),
            )(*ins)

        basis_shapes = [wide, wide, tall, wide, state]
        (f0,) = call(
            functools.partial(begin, rows_n, first),
            [rhs, u, v, a_vals, b_vals],
            [],
            [square],
            loads + basis_work + work + [pltpu.SemaphoreType.DMA((5,))],
            "begin",
        )

        def advance(t, down, left, state_in, coup_b):
            uk, utk, vk, vl, inverse = basis
            (y,) = call(
                functools.partial(take_left, rows_n, first + t + 1),
                [],
                [left, state_in, coup_b, utk, vk],
                [state],
                work,
                f"left{t}",
            )
            return call(
                functools.partial(finish_solve, rows_n, first + t + 1),
                [],
                [down, y, coup, uk, vk, vl, inverse],
                [square],
                work,
                f"solve{t}",
            )

        down = move(f0, up(0, 1))
        left = move(f0, right(0, 1))
        down_far = move(f0, up(0, 2))
        left_far = move(f0, right(0, 2))
        far0 = spread(ops0, cols_n, f0, "a", call)
        *basis, coup, s, a0, b0, a1, b1, a2, b2 = call(
            functools.partial(prepare, rows_n, first),
            [rhs, a_c, b_c, u, v, a_vals, b_vals],
            [],
            basis_shapes + [wide, state] + [square] * 6,
            loads[1:] + [pltpu.VMEM((2 * n, n), half), pltpu.SemaphoreType.DMA((9,))],
            "prepare",
        )
        (f1,) = advance(0, down, left, s, b0)
        down = move(f1, up(1, 1))
        left = move(f1, right(1, 1))
        (s1,) = call(
            functools.partial(third_early, rows_n, first),
            [],
            [down_far, left_far, s, a0, b0],
            [state],
            [],
            "third_early",
        )
        far1 = spread(ops1, cols_n, f1, "b", call)
        (f2,) = advance(1, down, left, s1, b1)
        for k, (ops, far, a, b) in enumerate(((ops0, far0, a0, b0), (ops1, far1, a1, b1))):
            (s,) = call(
                functools.partial(middle, rows_n, cols_n, first, ops),
                [],
                [s, a, b, *far],
                [state],
                [pltpu.VMEM((n, n), half)],
                f"middle{k}",
            )
        lasts = spread(ops2, cols_n, f2, "c", call)
        sent = [k for k, op in enumerate(ops2) if any(kind == "down" for _, _, kind, _ in op)]
        (s3,) = call(
            functools.partial(downs, cols_n, first, rows_n, [ops2[k] for k in sent]),
            [],
            [s, a2, *[lasts[k] for k in sent]],
            [state],
            [pltpu.VMEM((n, n), half)],
            "downs",
        )
        (out,) = call(
            functools.partial(publish, rows_n, first),
            [],
            [f0, f1, f2],
            [square],
            [pltpu.VMEM((n, n), half), pltpu.SemaphoreType.DMA],
            "publish",
        )
        (nxt,) = call(
            functools.partial(finish, rows_n, cols_n, first, ops2),
            [],
            [s3, b2, *lasts],
            [state],
            [pltpu.VMEM((n, n), half), pltpu.VMEM((n, n), full), pltpu.SemaphoreType.DMA((3,))],
            "finish",
        )
        return out, nxt

    placed = (
        P("row", "col"),
        P(None, "row", "col"),
        P(None, "row", "col"),
        P("row", None),
        P("col", None),
        P("row"),
        P("col"),
    )
    return jax.shard_map(
        shards,
        mesh=mesh,
        in_specs=placed,
        out_specs=(P("row", "col"), P("row", "col")),
        check_vma=False,
    )
```

```python
import functools

import jax
import jax.numpy as jnp
from jax import lax
from jax.experimental import pallas as pl
from jax.experimental.pallas import tpu as pltpu
from jax.sharding import PartitionSpec as P


AXES = ("row", "col")
VMEM_SPEC = pl.BlockSpec(memory_space=pltpu.VMEM)
FAR_SPEC = pl.BlockSpec(memory_space=pltpu.HBM)


def plan(rows_n, cols_n, offset, gap, up_gap, apart=False):
    rights, ups, last = [], [], []
    for i in range(rows_n):
        m = i + offset
        if 0 <= m < cols_n:
            targets = range(m + gap, cols_n)
            for chip in sorted({j // 2 for j in targets}, reverse=True):
                some = [(i, j) for j in targets if j // 2 == chip]
                (last if chip == m // 2 else rights).append(((i, m), some, "left"))
            ups += [((i, m), [(k, m)], "down") for k in range(i - up_gap + 1)]
    todo = rights + ups + last
    ops, forwards = [], []
    while todo:
        used_from, used_to, op = set(), set(), []
        allowed = {"left", "down"}
        if apart:
            turn = {kind for _, _, kind in todo}
            allowed = turn if len(turn) == 1 else {"left" if len(ops) % 2 == 0 else "down"}
        busy = [source for source, _, _ in todo]
        waiting = {targets[0]: busy.count(source) for source, targets, kind in todo if kind == "down"}
        for item in list(todo):
            source, targets, kind = item
            if kind not in allowed:
                continue
            for target in sorted(targets, key=lambda t: (waiting.get(t, 0), -t[1])):
                if source not in used_from and target not in used_to:
                    used_from.add(source)
                    used_to.add(target)
                    op.append((source, target, kind, None))
                    todo.remove(item)
                    forwards += [(target, other, kind, len(ops)) for other in targets if other != target]
                    break
        ops.append(op)
    return ops + [forwards] if forwards else ops


def one_of(me, ids):
    hit = me < 0
    for each in sorted(ids):
        hit = hit | (me == each)
    return hit


def place(cols_n):
    return lax.axis_index("row") * cols_n + lax.axis_index("col")


def level_of(rows_n):
    return rows_n - 1 - lax.axis_index("row") + lax.axis_index("col")


def dot(a, b):
    return lax.dot_general(a, b, (((1,), (0,)), ((), ())), preferred_element_type=jnp.float32)


def split(x):
    high = x.astype(jnp.bfloat16)
    return high, (x - high.astype(jnp.float32)).astype(jnp.bfloat16)


def put_left(ref, pair):
    n = pair[0].shape[1]
    ref[:, 0:n] = pair[0]
    ref[:, n : 2 * n] = pair[0]
    ref[:, 2 * n : 3 * n] = pair[1]


def put_right(ref, pair):
    n = pair[0].shape[0]
    ref[0:n] = pair[0]
    ref[n : 2 * n] = pair[1]
    ref[2 * n : 3 * n] = pair[0]


def dot_t(a, b):
    return lax.dot_general(a, b, (((1,), (1,)), ((), ())), preferred_element_type=jnp.float32)


def spectral(state, utk, vk, lhs, mid):
    put_left(lhs, split(state))
    part = dot(lhs[...], vk[...])
    put_right(mid, split(part))
    return dot(utk[...], mid[...])


def back(part, uk, vl, lhs, mid):
    put_left(lhs, split(part))
    part = dot_t(lhs[...], vl[...])
    put_right(mid, split(part))
    return dot(uk[...], mid[...]).astype(jnp.bfloat16)


def put_lanes(ref, pair):
    n = pair[0].shape[1]
    ref[:, 0:n] = pair[0]
    ref[:, n : 2 * n] = pair[1]
    ref[:, 2 * n : 3 * n] = pair[0]


def set_inverse(inverse, av, bv):
    n = inverse.shape[0]
    alpha = jnp.transpose(jnp.broadcast_to(av[...][None, :], (128, n)))
    beta = bv[...][None, :]
    for c in range(0, n, 128):
        inverse[:, c : c + 128] = 1.0 / (alpha + beta[:, c : c + 128])


def set_right_basis(v, vk, vl):
    pair = split(v[...])
    put_right(vk, pair)
    put_lanes(vl, pair)


def set_left_basis(u, uk, utk):
    high, low = split(u[...])
    put_left(uk, (high, low))
    put_left(utk, (high.T, low.T))


def copies(pairs, sem):
    moves = [pltpu.make_async_copy(source, target, sem.at[n]) for n, (source, target) in enumerate(pairs)]
    for move in moves:
        move.start()
    return moves


def begin(rows_n, first, rhs, u_far, v_far, a_vals, b_vals, f0, s, u, v, av, bv, uk, utk, vk, vl, inverse, lhs, mid, sem):
    @pl.when(level_of(rows_n) == first)
    def _():
        moves = copies(((v_far, v), (rhs, s), (u_far, u), (a_vals, av), (b_vals, bv)), sem)
        moves[0].wait()
        set_right_basis(v, vk, vl)
        for move in moves[1:]:
            move.wait()
        set_left_basis(u, uk, utk)
        set_inverse(inverse, av, bv)
        part = spectral(s[...], utk, vk, lhs, mid) * inverse[...]
        f0[...] = back(part, uk, vl, lhs, mid)


def prepare(rows_n, first, rhs, a_c, b_c, u_far, v_far, a_vals, b_vals, uk, utk, vk, vl, inverse, coup, s, a0, b0, a1, b1, a2, b2, u, v, av, bv, both, sem):
    level = level_of(rows_n)
    terms = ((rhs, s), (a_c.at[0], a0), (b_c.at[0], b0), (a_c.at[1], a1), (b_c.at[1], b1))

    @pl.when((level > first) & (level <= first + 2))
    def _():
        moves = copies(((v_far, v), (u_far, u), (a_vals, av), (b_vals, bv), *terms), sem)
        moves[0].wait()
        set_right_basis(v, vk, vl)
        moves[1].wait()
        set_left_basis(u, uk, utk)
        moves[2].wait()
        moves[3].wait()
        set_inverse(inverse, av, bv)
        for move in moves[4:]:
            move.wait()
        n = u.shape[0]
        for t, a in enumerate((a0, a1)):

            @pl.when(level == first + 1 + t)
            def _():
                both[0:n] = a[...]
                both[n:] = a[...]

        put_left(coup, split(dot(utk[:, n:], both[...])))

    @pl.when(level > first + 2)
    def _():
        for move in copies((*terms, (a_c.at[2], a2), (b_c.at[2], b2)), sem):
            move.wait()


def late(t):
    return (lax.rem(lax.axis_index("col"), 2) == 0) & (t == 1)


def take_left(rows_n, first, t, left, s, coup_b, utk, vk, out, lhs, mid):
    mine = level_of(rows_n) == first + t + 1

    @pl.when(mine)
    def _():
        out[...] = s[...] - dot(left[...], coup_b[...])

    @pl.when(mine & jnp.logical_not(late(t)))
    def _():
        out[...] = spectral(out[...], utk, vk, lhs, mid)


def finish_solve(rows_n, first, t, down, y, coup, coup_a, uk, utk, vk, vl, inverse, f, lhs, mid, part):
    mine = level_of(rows_n) == first + t + 1

    @pl.when(mine & late(t))
    def _():
        part[...] = spectral(y[...] - dot(coup_a[...], down[...]), utk, vk, lhs, mid) * inverse[...]

    @pl.when(mine & jnp.logical_not(late(t)))
    def _():
        n = y.shape[0]
        lhs[:, 0:n] = down[...]
        lhs[:, n : 2 * n] = down[...]
        put_right(mid, split(dot(lhs[:, 0 : 2 * n], vk[0 : 2 * n])))
        part[...] = (y[...] - dot(coup[...], mid[...])) * inverse[...]

    @pl.when(mine)
    def _():
        f[...] = back(part[...], uk, vl, lhs, mid)


def third_early(rows_n, first, down, left, s, a0, b0, s1):
    @pl.when(level_of(rows_n) == first + 2)
    def _():
        s1[...] = s[...] - (dot(a0[...], down[...]) + dot(left[...], b0[...]))


def subtract(cols_n, ops, arrived, got, state, coup_a, coup_b, out, kinds=("down", "left")):
    out[...] = state[...]
    for kind in kinds:
        hits = pick(cols_n, ops, kind, arrived, got)

        @pl.when(hits)
        def _():
            out[...] -= dot(got[...], coup_b[...]) if kind == "left" else dot(coup_a[...], got[...])


def middle(rows_n, cols_n, first, ops, s1, a1, b1, *rest):
    arrived, (s2, got) = rest[: len(ops)], rest[len(ops) :]

    @pl.when(level_of(rows_n) > first + 2)
    def _():
        subtract(cols_n, ops, arrived, got, s1, a1, b1, s2)


def pick(cols_n, ops, kind, arrived, got):
    me = place(cols_n)
    any_hit = me < 0
    for op, ref in zip(ops, arrived):
        hit = one_of(me, [t[0] * cols_n + t[1] for _, t, k, _ in op if k == kind])
        any_hit = any_hit | hit

        @pl.when(hit)
        def _():
            got[...] = ref[...]

    return any_hit


def downs(cols_n, first, rows_n, ops, s2, a2, *rest):
    arrived, (s3, got) = rest[: len(ops)], rest[len(ops) :]

    @pl.when(level_of(rows_n) > first + 2)
    def _():
        subtract(cols_n, ops, arrived, got, s2, a2, None, s3, ("down",))


def publish(rows_n, first, f0, f1, f2, out, zeros, sem):
    level = level_of(rows_n)
    for t, block in enumerate((f0, f1, f2)):

        @pl.when(level == first + t)
        def _():
            pltpu.make_async_copy(block, out, sem).start()

    @pl.when((level < first) | (level > first + 2))
    def _():
        zeros[...] = jnp.zeros(zeros.shape, zeros.dtype)
        pltpu.make_async_copy(zeros, out, sem).start()

    pltpu.make_async_copy(zeros, out, sem).wait()


def finish(rows_n, cols_n, first, ops, s3, b2, *rest):
    arrived, (nxt, got, mine, sem) = rest[: len(ops)], rest[len(ops) :]
    n = s3.shape[0]
    step = n // 3
    active = level_of(rows_n) > first + 2

    @pl.when(jnp.logical_not(active))
    def _():
        mine[...] = jnp.zeros(mine.shape, mine.dtype)
        for k in range(3):
            pltpu.make_async_copy(mine.at[pl.ds(k * step, step)], nxt.at[pl.ds(k * step, step)], sem.at[k]).start()

    @pl.when(active)
    def _():
        pick(cols_n, ops, "left", arrived, got)
        for k in range(3):
            rows = pl.ds(k * step, step)
            mine[rows] = s3[rows] - dot(got[rows], b2[...])
            pltpu.make_async_copy(mine.at[rows], nxt.at[rows], sem.at[k]).start()

    for k in range(3):
        pltpu.make_async_copy(mine.at[pl.ds(k * step, step)], nxt.at[pl.ds(k * step, step)], sem.at[k]).wait()


def relay(cols_n, choices, own, *rest):
    *arrived, out = rest
    me = place(cols_n)
    hit = me < 0
    for ids, ref in zip(choices, arrived):
        mine = one_of(me, ids)
        hit = hit | mine

        @pl.when(mine)
        def _():
            out[...] = ref[...]

    @pl.when(jnp.logical_not(hit))
    def _():
        out[...] = own[...]


def spread(ops, cols_n, own, name, call):
    arrived = []
    for k, op in enumerate(ops):
        value = own
        earlier = sorted({f for *_, f in op if f is not None})
        if earlier:
            choices = [[s[0] * cols_n + s[1] for s, _, _, f in op if f == e] for e in earlier]
            (value,) = call(
                functools.partial(relay, cols_n, choices),
                [],
                [own, *[arrived[e] for e in earlier]],
                [jax.ShapeDtypeStruct(own.shape, own.dtype)],
                [],
                f"relay_{name}{k}",
            )
        pairs = [(s[0] * cols_n + s[1], t[0] * cols_n + t[1]) for s, t, _, _ in op]
        arrived.append(move(value, pairs))
    return arrived


def move(value, pairs):
    return lax.ppermute(value, AXES, pairs)


def solution(mesh):
    rows_n, cols_n = mesh.shape["row"], mesh.shape["col"]
    first = (rows_n + cols_n) // 2 - 2
    offset = first - rows_n + 1
    ops0 = plan(rows_n, cols_n, offset, 3, 3)
    ops1 = plan(rows_n, cols_n, offset + 1, 2, 2)
    ops2 = plan(rows_n, cols_n, offset + 2, 1, 1, True)

    def owners(t):
        return [(i, i + offset + t) for i in range(rows_n) if 0 <= i + offset + t < cols_n]

    def up(t, far):
        return [(i * cols_n + j, (i - far) * cols_n + j) for i, j in owners(t) if i >= far]

    def right(t, far):
        return [(i * cols_n + j, i * cols_n + j + far) for i, j in owners(t) if j + far < cols_n]

    def shards(rhs, a_c, b_c, u, v, a_vals, b_vals):
        n = rhs.shape[0]
        half, full = jnp.bfloat16, jnp.float32
        square = jax.ShapeDtypeStruct((n, n), half)
        wide, tall = jax.ShapeDtypeStruct((n, 3 * n), half), jax.ShapeDtypeStruct((3 * n, n), half)
        state = jax.ShapeDtypeStruct((n, n), full)
        loads = [pltpu.VMEM((n, n), full)] * 3 + [pltpu.VMEM((n,), full)] * 2
        basis_work = [pltpu.VMEM((n, 3 * n), half)] * 2 + [pltpu.VMEM((3 * n, n), half), pltpu.VMEM((n, 3 * n), half), pltpu.VMEM((n, n), full)]
        work = [pltpu.VMEM((n, 3 * n), half), pltpu.VMEM((3 * n, n), half)]

        def call(kernel, far, near, outs, scratch, name):
            ins = [pltpu.with_memory_space_constraint(x, pltpu.HBM) for x in far] + list(near)
            return pl.pallas_call(
                kernel,
                out_shape=outs,
                in_specs=[FAR_SPEC] * len(far) + [VMEM_SPEC] * len(near),
                out_specs=[FAR_SPEC if name in ("finish", "publish") else VMEM_SPEC] * len(outs),
                scratch_shapes=scratch,
                compiler_params=pltpu.CompilerParams(vmem_limit_bytes=24 << 20),
            )(*ins)

        basis_shapes = [wide, wide, tall, wide, state]
        (f0,) = call(
            functools.partial(begin, rows_n, first),
            [rhs, u, v, a_vals, b_vals],
            [],
            [square],
            loads + basis_work + work + [pltpu.SemaphoreType.DMA((5,))],
            "begin",
        )

        def advance(t, down, left, state_in, coup_a, coup_b):
            _, utk, vk, _, _ = basis
            (y,) = call(
                functools.partial(take_left, rows_n, first, t),
                [],
                [left, state_in, coup_b, utk, vk],
                [state],
                work,
                f"left{t}",
            )
            return call(
                functools.partial(finish_solve, rows_n, first, t),
                [],
                [down, y, coup, coup_a, *basis],
                [square],
                work + [pltpu.VMEM((n, n), full)],
                f"solve{t}",
            )

        down = move(f0, up(0, 1))
        left = move(f0, right(0, 1))
        down_far = move(f0, up(0, 2))
        left_far = move(f0, right(0, 2))
        far0 = spread(ops0, cols_n, f0, "a", call)
        *basis, coup, s, a0, b0, a1, b1, a2, b2 = call(
            functools.partial(prepare, rows_n, first),
            [rhs, a_c, b_c, u, v, a_vals, b_vals],
            [],
            basis_shapes + [wide, state] + [square] * 6,
            loads[1:] + [pltpu.VMEM((2 * n, n), half), pltpu.SemaphoreType.DMA((9,))],
            "prepare",
        )
        (f1,) = advance(0, down, left, s, a0, b0)
        down = move(f1, up(1, 1))
        left = move(f1, right(1, 1))
        (s1,) = call(
            functools.partial(third_early, rows_n, first),
            [],
            [down_far, left_far, s, a0, b0],
            [state],
            [],
            "third_early",
        )
        far1 = spread(ops1, cols_n, f1, "b", call)
        (f2,) = advance(1, down, left, s1, a1, b1)
        for k, (ops, far, a, b) in enumerate(((ops0, far0, a0, b0), (ops1, far1, a1, b1))):
            (s,) = call(
                functools.partial(middle, rows_n, cols_n, first, ops),
                [],
                [s, a, b, *far],
                [state],
                [pltpu.VMEM((n, n), half)],
                f"middle{k}",
            )
        lasts = spread(ops2, cols_n, f2, "c", call)
        sent = [k for k, op in enumerate(ops2) if any(kind == "down" for _, _, kind, _ in op)]
        (s3,) = call(
            functools.partial(downs, cols_n, first, rows_n, [ops2[k] for k in sent]),
            [],
            [s, a2, *[lasts[k] for k in sent]],
            [state],
            [pltpu.VMEM((n, n), half)],
            "downs",
        )
        (out,) = call(
            functools.partial(publish, rows_n, first),
            [],
            [f0, f1, f2],
            [square],
            [pltpu.VMEM((n, n), half), pltpu.SemaphoreType.DMA],
            "publish",
        )
        (nxt,) = call(
            functools.partial(finish, rows_n, cols_n, first, ops2),
            [],
            [s3, b2, *lasts],
            [state],
            [pltpu.VMEM((n, n), half), pltpu.VMEM((n, n), full), pltpu.SemaphoreType.DMA((3,))],
            "finish",
        )
        return out, nxt

    placed = (
        P("row", "col"),
        P(None, "row", "col"),
        P(None, "row", "col"),
        P("row", None),
        P("col", None),
        P("row"),
        P("col"),
    )
    return jax.shard_map(
        shards,
        mesh=mesh,
        in_specs=placed,
        out_specs=(P("row", "col"), P("row", "col")),
        check_vma=False,
    )
```

```python
import functools

import jax
import jax.numpy as jnp
from jax import lax
from jax.experimental import pallas as pl
from jax.experimental.pallas import tpu as pltpu
from jax.sharding import PartitionSpec as P


AXES = ("row", "col")
VMEM_SPEC = pl.BlockSpec(memory_space=pltpu.VMEM)
FAR_SPEC = pl.BlockSpec(memory_space=pltpu.HBM)


def plan(rows_n, cols_n, offset, gap, up_gap, apart=False):
    rights, ups, last = [], [], []
    for i in range(rows_n):
        m = i + offset
        if 0 <= m < cols_n:
            targets = range(m + gap, cols_n)
            for chip in sorted({j // 2 for j in targets}, reverse=True):
                some = [(i, j) for j in targets if j // 2 == chip]
                (last if chip == m // 2 else rights).append(((i, m), some, "left"))
            ups += [((i, m), [(k, m)], "down") for k in range(i - up_gap + 1)]
    todo = rights + ups + last
    ops, forwards = [], []
    while todo:
        used_from, used_to, op = set(), set(), []
        allowed = {"left", "down"}
        if apart:
            turn = {kind for _, _, kind in todo}
            allowed = turn if len(turn) == 1 else {"down" if 0 < len(ops) < 4 else "left"}
        busy = [source for source, _, _ in todo]
        waiting = {targets[0]: busy.count(source) for source, targets, kind in todo if kind == "down"}
        for item in list(todo):
            source, targets, kind = item
            if kind not in allowed:
                continue
            for target in sorted(targets, key=lambda t: (waiting.get(t, 0), -t[1])):
                if source not in used_from and target not in used_to:
                    used_from.add(source)
                    used_to.add(target)
                    op.append((source, target, kind, None))
                    todo.remove(item)
                    forwards += [(target, other, kind, len(ops)) for other in targets if other != target]
                    break
        ops.append(op)
    return ops + [forwards] if forwards else ops


def chain(rows_n, cols_n, offset):
    first, steps, ups = [], [], []
    for i in range(rows_n):
        m = i + offset
        if not 0 <= m < cols_n:
            continue
        chips = {}
        for j in range(m + 3, cols_n):
            if j // 2 != (m + 2) // 2:
                chips.setdefault(j // 2, []).append((i, j))
        leads = [max(chips[chip]) for chip in sorted(chips)]
        for n, lead in enumerate(leads):
            if n == 0:
                first.append(((i, m), lead, "left", None))
            mates = [t for t in chips[lead[1] // 2] if t != lead]
            onward = leads[n + 1 : n + 2]
            for k, target in enumerate(onward + mates):
                while len(steps) < n + k + 1:
                    steps.append([])
                steps[n + k].append((lead, target))
        ups += [((i, m), (k, m), "down", None) for k in range(i - 2)]
    ops = [first]
    for edge in ups:
        for op in ops + [[]]:
            if all(edge[0] != other[0] and edge[1] != other[1] for other in op):
                if not op:
                    ops.append(op)
                op.append(edge)
                break
    came = {target: 0 for _, target, _, _ in first}
    for step in steps:
        came.update({target: len(ops) for _, target in step if target not in came})
        ops.append([(lead, target, "left", came[lead]) for lead, target in step])
    return ops


def one_of(me, ids):
    hit = me < 0
    for each in sorted(ids):
        hit = hit | (me == each)
    return hit


def place(cols_n):
    return lax.axis_index("row") * cols_n + lax.axis_index("col")


def level_of(rows_n):
    return rows_n - 1 - lax.axis_index("row") + lax.axis_index("col")


def dot(a, b):
    return lax.dot_general(a, b, (((1,), (0,)), ((), ())), preferred_element_type=jnp.float32)


def split(x):
    high = x.astype(jnp.bfloat16)
    return high, (x - high.astype(jnp.float32)).astype(jnp.bfloat16)


def put_left(ref, pair):
    n = pair[0].shape[1]
    ref[:, 0:n] = pair[0]
    ref[:, n : 2 * n] = pair[0]
    ref[:, 2 * n : 3 * n] = pair[1]


def put_right(ref, pair):
    n = pair[0].shape[0]
    ref[0:n] = pair[0]
    ref[n : 2 * n] = pair[1]
    ref[2 * n : 3 * n] = pair[0]


def dot_t(a, b):
    return lax.dot_general(a, b, (((1,), (1,)), ((), ())), preferred_element_type=jnp.float32)


def spectral(state, utk, vk, lhs, mid):
    put_left(lhs, split(state))
    part = dot(lhs[...], vk[...])
    put_right(mid, split(part))
    return dot(utk[...], mid[...])


def back(part, uk, vl, lhs, mid):
    put_left(lhs, split(part))
    part = dot_t(lhs[...], vl[...])
    put_right(mid, split(part))
    return dot(uk[...], mid[...]).astype(jnp.bfloat16)


def put_lanes(ref, pair):
    n = pair[0].shape[1]
    ref[:, 0:n] = pair[0]
    ref[:, n : 2 * n] = pair[1]
    ref[:, 2 * n : 3 * n] = pair[0]


def set_inverse(inverse, av, bv):
    n = inverse.shape[0]
    alpha = jnp.transpose(jnp.broadcast_to(av[...][None, :], (128, n)))
    beta = bv[...][None, :]
    for c in range(0, n, 128):
        inverse[:, c : c + 128] = 1.0 / (alpha + beta[:, c : c + 128])


def set_right_basis(v, vk, vl):
    pair = split(v[...])
    put_right(vk, pair)
    put_lanes(vl, pair)


def set_left_basis(u, uk, utk):
    high, low = split(u[...])
    put_left(uk, (high, low))
    put_left(utk, (high.T, low.T))


def copies(pairs, sem):
    moves = [pltpu.make_async_copy(source, target, sem.at[n]) for n, (source, target) in enumerate(pairs)]
    for move in moves:
        move.start()
    return moves


def begin(rows_n, first, rhs, u_far, v_far, a_vals, b_vals, f0, s, u, v, av, bv, uk, utk, vk, vl, inverse, lhs, mid, sem):
    @pl.when(level_of(rows_n) == first)
    def _():
        moves = copies(((v_far, v), (rhs, s), (u_far, u), (a_vals, av), (b_vals, bv)), sem)
        moves[0].wait()
        set_right_basis(v, vk, vl)
        for move in moves[1:]:
            move.wait()
        set_left_basis(u, uk, utk)
        set_inverse(inverse, av, bv)
        part = spectral(s[...], utk, vk, lhs, mid) * inverse[...]
        f0[...] = back(part, uk, vl, lhs, mid)


def prepare(rows_n, first, rhs, a_c, b_c, u_far, v_far, a_vals, b_vals, uk, utk, vk, vl, inverse, coup, s, a0, b0, a1, b1, a2, b2, u, v, av, bv, both, sem):
    level = level_of(rows_n)
    terms = ((rhs, s), (a_c.at[0], a0), (b_c.at[0], b0), (a_c.at[1], a1), (b_c.at[1], b1))

    @pl.when((level > first) & (level <= first + 2))
    def _():
        moves = copies(((v_far, v), (u_far, u), (a_vals, av), (b_vals, bv), *terms), sem)
        moves[0].wait()
        set_right_basis(v, vk, vl)
        moves[1].wait()
        set_left_basis(u, uk, utk)
        moves[2].wait()
        moves[3].wait()
        set_inverse(inverse, av, bv)
        for move in moves[4:]:
            move.wait()
        n = u.shape[0]
        for t, a in enumerate((a0, a1)):

            @pl.when(level == first + 1 + t)
            def _():
                both[0:n] = a[...]
                both[n:] = a[...]

        put_left(coup, split(dot(utk[:, n:], both[...])))

    @pl.when(level > first + 2)
    def _():
        for move in copies((*terms, (a_c.at[2], a2), (b_c.at[2], b2)), sem):
            move.wait()


def late(t):
    return (lax.rem(lax.axis_index("col"), 2) == 0) & (t == 1)


def take_left(rows_n, first, t, left, s, coup_b, utk, vk, out, lhs, mid):
    mine = level_of(rows_n) == first + t + 1

    @pl.when(mine)
    def _():
        out[...] = s[...] - dot(left[...], coup_b[...])

    @pl.when(mine & jnp.logical_not(late(t)))
    def _():
        out[...] = spectral(out[...], utk, vk, lhs, mid)


def finish_solve(rows_n, first, t, down, y, coup, coup_a, uk, utk, vk, vl, inverse, f, lhs, mid, part):
    mine = level_of(rows_n) == first + t + 1

    @pl.when(mine & late(t))
    def _():
        part[...] = spectral(y[...] - dot(coup_a[...], down[...]), utk, vk, lhs, mid) * inverse[...]

    @pl.when(mine & jnp.logical_not(late(t)))
    def _():
        n = y.shape[0]
        lhs[:, 0:n] = down[...]
        lhs[:, n : 2 * n] = down[...]
        put_right(mid, split(dot(lhs[:, 0 : 2 * n], vk[0 : 2 * n])))
        part[...] = (y[...] - dot(coup[...], mid[...])) * inverse[...]

    @pl.when(mine)
    def _():
        f[...] = back(part[...], uk, vl, lhs, mid)


def third_early(rows_n, first, down, left, s, a0, b0, s1):
    @pl.when(level_of(rows_n) == first + 2)
    def _():
        s1[...] = s[...] - (dot(a0[...], down[...]) + dot(left[...], b0[...]))


def subtract(cols_n, ops, arrived, got, state, coup_a, coup_b, out, kinds=("down", "left")):
    out[...] = state[...]
    for kind in kinds:
        hits = pick(cols_n, ops, kind, arrived, got)

        @pl.when(hits)
        def _():
            out[...] -= dot(got[...], coup_b[...]) if kind == "left" else dot(coup_a[...], got[...])


def middle(rows_n, cols_n, first, ops, s1, a1, b1, *rest):
    arrived, (s2, got) = rest[: len(ops)], rest[len(ops) :]

    @pl.when(level_of(rows_n) > first + 2)
    def _():
        subtract(cols_n, ops, arrived, got, s1, a1, b1, s2)


def pick(cols_n, ops, kind, arrived, got):
    me = place(cols_n)
    any_hit = me < 0
    for op, ref in zip(ops, arrived):
        hit = one_of(me, [t[0] * cols_n + t[1] for _, t, k, _ in op if k == kind])
        any_hit = any_hit | hit

        @pl.when(hit)
        def _():
            got[...] = ref[...]

    return any_hit


def downs(cols_n, first, rows_n, ops, s2, a2, *rest):
    arrived, (s3, got) = rest[: len(ops)], rest[len(ops) :]

    @pl.when(level_of(rows_n) > first + 2)
    def _():
        subtract(cols_n, ops, arrived, got, s2, a2, None, s3, ("down",))


def publish(rows_n, first, f0, f1, f2, out, zeros, sem):
    level = level_of(rows_n)
    for t, block in enumerate((f0, f1, f2)):

        @pl.when(level == first + t)
        def _():
            pltpu.make_async_copy(block, out, sem).start()

    @pl.when((level < first) | (level > first + 2))
    def _():
        zeros[...] = jnp.zeros(zeros.shape, zeros.dtype)
        pltpu.make_async_copy(zeros, out, sem).start()

    pltpu.make_async_copy(zeros, out, sem).wait()


def finish(rows_n, cols_n, first, ops, s3, b2, *rest):
    arrived, (nxt, got, mine, sem) = rest[: len(ops)], rest[len(ops) :]
    n = s3.shape[0]
    step = n // 3
    active = level_of(rows_n) > first + 2

    @pl.when(jnp.logical_not(active))
    def _():
        mine[...] = jnp.zeros(mine.shape, mine.dtype)
        for k in range(3):
            pltpu.make_async_copy(mine.at[pl.ds(k * step, step)], nxt.at[pl.ds(k * step, step)], sem.at[k]).start()

    @pl.when(active)
    def _():
        pick(cols_n, ops, "left", arrived, got)
        for k in range(3):
            rows = pl.ds(k * step, step)
            mine[rows] = s3[rows] - dot(got[rows], b2[...])
            pltpu.make_async_copy(mine.at[rows], nxt.at[rows], sem.at[k]).start()

    for k in range(3):
        pltpu.make_async_copy(mine.at[pl.ds(k * step, step)], nxt.at[pl.ds(k * step, step)], sem.at[k]).wait()


def relay(cols_n, choices, own, *rest):
    *arrived, out = rest
    me = place(cols_n)
    hit = me < 0
    for ids, ref in zip(choices, arrived):
        mine = one_of(me, ids)
        hit = hit | mine

        @pl.when(mine)
        def _():
            out[...] = ref[...]

    @pl.when(jnp.logical_not(hit))
    def _():
        out[...] = own[...]


def spread(ops, cols_n, own, name, call):
    arrived = []
    for k, op in enumerate(ops):
        value = own
        earlier = sorted({f for *_, f in op if f is not None})
        if earlier:
            choices = [[s[0] * cols_n + s[1] for s, _, _, f in op if f == e] for e in earlier]
            (value,) = call(
                functools.partial(relay, cols_n, choices),
                [],
                [own, *[arrived[e] for e in earlier]],
                [jax.ShapeDtypeStruct(own.shape, own.dtype)],
                [],
                f"relay_{name}{k}",
            )
        pairs = [(s[0] * cols_n + s[1], t[0] * cols_n + t[1]) for s, t, _, _ in op]
        arrived.append(move(value, pairs))
    return arrived


def move(value, pairs):
    return lax.ppermute(value, AXES, pairs)


def solution(mesh):
    rows_n, cols_n = mesh.shape["row"], mesh.shape["col"]
    first = (rows_n + cols_n) // 2 - 2
    offset = first - rows_n + 1
    ops0 = chain(rows_n, cols_n, offset)
    ops1 = plan(rows_n, cols_n, offset + 1, 2, 2)
    ops2 = plan(rows_n, cols_n, offset + 2, 1, 1, True)

    def owners(t):
        return [(i, i + offset + t) for i in range(rows_n) if 0 <= i + offset + t < cols_n]

    beside = [
        ((i, j + 2), (i, j + 3), "left", None) for i, j in owners(0) if (j + 2) % 2 == 0 and j + 3 < cols_n
    ]

    def up(t, far):
        return [(i * cols_n + j, (i - far) * cols_n + j) for i, j in owners(t) if i >= far]

    def right(t, far):
        return [(i * cols_n + j, i * cols_n + j + far) for i, j in owners(t) if j + far < cols_n]

    def shards(rhs, a_c, b_c, u, v, a_vals, b_vals):
        n = rhs.shape[0]
        half, full = jnp.bfloat16, jnp.float32
        square = jax.ShapeDtypeStruct((n, n), half)
        wide, tall = jax.ShapeDtypeStruct((n, 3 * n), half), jax.ShapeDtypeStruct((3 * n, n), half)
        state = jax.ShapeDtypeStruct((n, n), full)
        loads = [pltpu.VMEM((n, n), full)] * 3 + [pltpu.VMEM((n,), full)] * 2
        basis_work = [pltpu.VMEM((n, 3 * n), half)] * 2 + [pltpu.VMEM((3 * n, n), half), pltpu.VMEM((n, 3 * n), half), pltpu.VMEM((n, n), full)]
        work = [pltpu.VMEM((n, 3 * n), half), pltpu.VMEM((3 * n, n), half)]

        def call(kernel, far, near, outs, scratch, name):
            ins = [pltpu.with_memory_space_constraint(x, pltpu.HBM) for x in far] + list(near)
            return pl.pallas_call(
                kernel,
                out_shape=outs,
                in_specs=[FAR_SPEC] * len(far) + [VMEM_SPEC] * len(near),
                out_specs=[FAR_SPEC if name in ("finish", "publish") else VMEM_SPEC] * len(outs),
                scratch_shapes=scratch,
                compiler_params=pltpu.CompilerParams(vmem_limit_bytes=24 << 20),
            )(*ins)

        basis_shapes = [wide, wide, tall, wide, state]
        (f0,) = call(
            functools.partial(begin, rows_n, first),
            [rhs, u, v, a_vals, b_vals],
            [],
            [square],
            loads + basis_work + work + [pltpu.SemaphoreType.DMA((5,))],
            "begin",
        )

        def advance(t, down, left, state_in, coup_a, coup_b):
            _, utk, vk, _, _ = basis
            (y,) = call(
                functools.partial(take_left, rows_n, first, t),
                [],
                [left, state_in, coup_b, utk, vk],
                [state],
                work,
                f"left{t}",
            )
            return call(
                functools.partial(finish_solve, rows_n, first, t),
                [],
                [down, y, coup, coup_a, *basis],
                [square],
                work + [pltpu.VMEM((n, n), full)],
                f"solve{t}",
            )

        down = move(f0, up(0, 1))
        left = move(f0, right(0, 1))
        down_far = move(f0, up(0, 2))
        left_far = move(f0, right(0, 2))
        far0 = spread(ops0, cols_n, f0, "a", call)
        far0.append(move(left_far, [(a[0] * cols_n + a[1], b[0] * cols_n + b[1]) for a, b, _, _ in beside]))
        *basis, coup, s, a0, b0, a1, b1, a2, b2 = call(
            functools.partial(prepare, rows_n, first),
            [rhs, a_c, b_c, u, v, a_vals, b_vals],
            [],
            basis_shapes + [wide, state] + [square] * 6,
            loads[1:] + [pltpu.VMEM((2 * n, n), half), pltpu.SemaphoreType.DMA((9,))],
            "prepare",
        )
        (f1,) = advance(0, down, left, s, a0, b0)
        down = move(f1, up(1, 1))
        left = move(f1, right(1, 1))
        (s1,) = call(
            functools.partial(third_early, rows_n, first),
            [],
            [down_far, left_far, s, a0, b0],
            [state],
            [],
            "third_early",
        )
        far1 = spread(ops1, cols_n, f1, "b", call)
        (f2,) = advance(1, down, left, s1, a1, b1)
        for k, (ops, far, a, b) in enumerate(((ops0 + [beside], far0, a0, b0), (ops1, far1, a1, b1))):
            (s,) = call(
                functools.partial(middle, rows_n, cols_n, first, ops),
                [],
                [s, a, b, *far],
                [state],
                [pltpu.VMEM((n, n), half)],
                f"middle{k}",
            )
        lasts = spread(ops2, cols_n, f2, "c", call)
        sent = [k for k, op in enumerate(ops2) if any(kind == "down" for _, _, kind, _ in op)]
        (s3,) = call(
            functools.partial(downs, cols_n, first, rows_n, [ops2[k] for k in sent]),
            [],
            [s, a2, *[lasts[k] for k in sent]],
            [state],
            [pltpu.VMEM((n, n), half)],
            "downs",
        )
        (out,) = call(
            functools.partial(publish, rows_n, first),
            [],
            [f0, f1, f2],
            [square],
            [pltpu.VMEM((n, n), half), pltpu.SemaphoreType.DMA],
            "publish",
        )
        (nxt,) = call(
            functools.partial(finish, rows_n, cols_n, first, ops2),
            [],
            [s3, b2, *lasts],
            [state],
            [pltpu.VMEM((n, n), half), pltpu.VMEM((n, n), full), pltpu.SemaphoreType.DMA((3,))],
            "finish",
        )
        return out, nxt

    placed = (
        P("row", "col"),
        P(None, "row", "col"),
        P(None, "row", "col"),
        P("row", None),
        P("col", None),
        P("row"),
        P("col"),
    )
    return jax.shard_map(
        shards,
        mesh=mesh,
        in_specs=placed,
        out_specs=(P("row", "col"), P("row", "col")),
        check_vma=False,
    )
```

```python
import functools

import jax
import jax.numpy as jnp
from jax import lax
from jax.experimental import pallas as pl
from jax.experimental.pallas import tpu as pltpu
from jax.sharding import PartitionSpec as P


AXES = ("row", "col")
VMEM_SPEC = pl.BlockSpec(memory_space=pltpu.VMEM)
FAR_SPEC = pl.BlockSpec(memory_space=pltpu.HBM)


def plan(rows_n, cols_n, offset, gap, up_gap, apart=False):
    rights, ups, last = [], [], []
    for i in range(rows_n):
        m = i + offset
        if 0 <= m < cols_n:
            targets = range(m + gap, cols_n)
            for chip in sorted({j // 2 for j in targets}, reverse=apart):
                some = [(i, j) for j in targets if j // 2 == chip]
                (last if chip == m // 2 else rights).append(((i, m), some, "left"))
            above = list(range(i - up_gap + 1))
            ups += [((i, m), [(k, m)], "down") for k in above[:1] + above[1:][-1:] + above[1:-1]]
    todo = rights + ups + last
    ops, forwards = [], []
    while todo:
        used_from, used_to, op = set(), set(), []
        allowed = {"left", "down"}
        if apart:
            turn = {kind for _, _, kind in todo}
            allowed = turn if len(turn) == 1 else {"down" if 0 < len(ops) < 4 else "left"}
        busy = [source for source, _, _ in todo]
        waiting = {targets[0]: busy.count(source) for source, targets, kind in todo if kind == "down"}
        for item in list(todo):
            source, targets, kind = item
            if kind not in allowed or (apart and not ops and item in last and rights):
                continue
            for target in sorted(targets, key=lambda t: (waiting.get(t, 0), -t[1])):
                if source not in used_from and target not in used_to:
                    used_from.add(source)
                    used_to.add(target)
                    op.append((source, target, kind, None))
                    todo.remove(item)
                    forwards += [(target, other, kind, len(ops)) for other in targets if other != target]
                    break
        ops.append(op)
    return ops + [forwards] if forwards else ops


def chain(rows_n, cols_n, offset):
    first, steps, ups = [], [], []
    for i in range(rows_n):
        m = i + offset
        if not 0 <= m < cols_n:
            continue
        chips = {}
        for j in range(m + 3, cols_n):
            if j // 2 != (m + 2) // 2:
                chips.setdefault(j // 2, []).append((i, j))
        leads = [max(chips[chip]) for chip in sorted(chips)]
        for n, lead in enumerate(leads):
            if n == 0:
                first.append(((i, m), lead, "left", None))
            mates = [t for t in chips[lead[1] // 2] if t != lead]
            onward = leads[n + 1 : n + 2]
            for k, target in enumerate(onward + mates):
                while len(steps) < n + k + 1:
                    steps.append([])
                steps[n + k].append((lead, target))
        ups += [((i, m), (k, m), "down", None) for k in range(i - 2)]
    ops = [first]
    for edge in ups:
        for op in ops + [[]]:
            if all(edge[0] != other[0] and edge[1] != other[1] for other in op):
                if not op:
                    ops.append(op)
                op.append(edge)
                break
    came = {target: 0 for _, target, _, _ in first}
    for step in steps:
        came.update({target: len(ops) for _, target in step if target not in came})
        ops.append([(lead, target, "left", came[lead]) for lead, target in step])
    return ops


def one_of(me, ids):
    hit = me < 0
    for each in sorted(ids):
        hit = hit | (me == each)
    return hit


def place(cols_n):
    return lax.axis_index("row") * cols_n + lax.axis_index("col")


def level_of(rows_n):
    return rows_n - 1 - lax.axis_index("row") + lax.axis_index("col")


def dot(a, b):
    return lax.dot_general(a, b, (((1,), (0,)), ((), ())), preferred_element_type=jnp.float32)


def split(x):
    high = x.astype(jnp.bfloat16)
    return high, (x - high.astype(jnp.float32)).astype(jnp.bfloat16)


def put_left(ref, pair):
    n = pair[0].shape[1]
    ref[:, 0:n] = pair[0]
    ref[:, n : 2 * n] = pair[0]
    ref[:, 2 * n : 3 * n] = pair[1]


def put_right(ref, pair):
    n = pair[0].shape[0]
    ref[0:n] = pair[0]
    ref[n : 2 * n] = pair[1]
    ref[2 * n : 3 * n] = pair[0]


def dot_t(a, b):
    return lax.dot_general(a, b, (((1,), (1,)), ((), ())), preferred_element_type=jnp.float32)


def spectral(state, utk, vk, lhs, mid):
    put_left(lhs, split(state))
    part = dot(lhs[...], vk[...])
    put_right(mid, split(part))
    return dot(utk[...], mid[...])


def back(part, uk, vl, lhs, mid):
    put_left(lhs, split(part))
    part = dot_t(lhs[...], vl[...])
    put_right(mid, split(part))
    return dot(uk[...], mid[...]).astype(jnp.bfloat16)


def put_lanes(ref, pair):
    n = pair[0].shape[1]
    ref[:, 0:n] = pair[0]
    ref[:, n : 2 * n] = pair[1]
    ref[:, 2 * n : 3 * n] = pair[0]


def set_inverse(inverse, av, bv):
    n = inverse.shape[0]
    alpha = jnp.transpose(jnp.broadcast_to(av[...][None, :], (128, n)))
    beta = bv[...][None, :]
    for c in range(0, n, 128):
        inverse[:, c : c + 128] = 1.0 / (alpha + beta[:, c : c + 128])


def set_right_basis(v, vk, vl):
    pair = split(v[...])
    put_right(vk, pair)
    put_lanes(vl, pair)


def set_left_basis(u, uk, utk):
    high, low = split(u[...])
    put_left(uk, (high, low))
    put_left(utk, (high.T, low.T))


def copies(pairs, sem):
    moves = [pltpu.make_async_copy(source, target, sem.at[n]) for n, (source, target) in enumerate(pairs)]
    for move in moves:
        move.start()
    return moves


def begin(rows_n, first, rhs, u_far, v_far, a_vals, b_vals, f0, s, u, v, av, bv, uk, utk, vk, vl, inverse, lhs, mid, sem):
    @pl.when(level_of(rows_n) == first)
    def _():
        moves = copies(((v_far, v), (rhs, s), (u_far, u), (a_vals, av), (b_vals, bv)), sem)
        moves[0].wait()
        set_right_basis(v, vk, vl)
        for move in moves[1:]:
            move.wait()
        set_left_basis(u, uk, utk)
        set_inverse(inverse, av, bv)
        part = spectral(s[...], utk, vk, lhs, mid) * inverse[...]
        f0[...] = back(part, uk, vl, lhs, mid)


def prepare(rows_n, first, rhs, a_c, b_c, u_far, v_far, a_vals, b_vals, uk, utk, vk, vl, inverse, coup, s, a0, b0, a1, b1, a2, b2, u, v, av, bv, both, sem):
    level = level_of(rows_n)
    terms = ((rhs, s), (a_c.at[0], a0), (b_c.at[0], b0), (a_c.at[1], a1), (b_c.at[1], b1))

    @pl.when((level > first) & (level <= first + 2))
    def _():
        moves = copies(((v_far, v), (u_far, u), (a_vals, av), (b_vals, bv), *terms), sem)
        moves[0].wait()
        set_right_basis(v, vk, vl)
        moves[1].wait()
        set_left_basis(u, uk, utk)
        moves[2].wait()
        moves[3].wait()
        set_inverse(inverse, av, bv)
        for move in moves[4:]:
            move.wait()
        n = u.shape[0]
        for t, a in enumerate((a0, a1)):

            @pl.when(level == first + 1 + t)
            def _():
                both[0:n] = a[...]
                both[n:] = a[...]

        put_left(coup, split(dot(utk[:, n:], both[...])))

    @pl.when(level > first + 2)
    def _():
        for move in copies((*terms, (a_c.at[2], a2), (b_c.at[2], b2)), sem):
            move.wait()


def late(t):
    return (lax.rem(lax.axis_index("col"), 2) == 0) & (t == 1)


def take_left(rows_n, first, t, left, s, coup_b, utk, vk, out, lhs, mid):
    mine = level_of(rows_n) == first + t + 1

    @pl.when(mine)
    def _():
        out[...] = s[...] - dot(left[...], coup_b[...])

    @pl.when(mine & jnp.logical_not(late(t)))
    def _():
        out[...] = spectral(out[...], utk, vk, lhs, mid)


def finish_solve(rows_n, first, t, down, y, coup, coup_a, uk, utk, vk, vl, inverse, f, lhs, mid, part):
    mine = level_of(rows_n) == first + t + 1

    @pl.when(mine & late(t))
    def _():
        part[...] = spectral(y[...] - dot(coup_a[...], down[...]), utk, vk, lhs, mid) * inverse[...]

    @pl.when(mine & jnp.logical_not(late(t)))
    def _():
        n = y.shape[0]
        lhs[:, 0:n] = down[...]
        lhs[:, n : 2 * n] = down[...]
        put_right(mid, split(dot(lhs[:, 0 : 2 * n], vk[0 : 2 * n])))
        part[...] = (y[...] - dot(coup[...], mid[...])) * inverse[...]

    @pl.when(mine)
    def _():
        f[...] = back(part[...], uk, vl, lhs, mid)


def third_early(rows_n, first, down, left, s, a0, b0, s1):
    @pl.when(level_of(rows_n) == first + 2)
    def _():
        s1[...] = s[...] - (dot(a0[...], down[...]) + dot(left[...], b0[...]))


def subtract(cols_n, ops, arrived, got, state, coup_a, coup_b, out, kinds=("down", "left")):
    out[...] = state[...]
    for kind in kinds:
        hits = pick(cols_n, ops, kind, arrived, got)

        @pl.when(hits)
        def _():
            out[...] -= dot(got[...], coup_b[...]) if kind == "left" else dot(coup_a[...], got[...])


def middle(rows_n, cols_n, first, ops, s1, a1, b1, *rest):
    arrived, (s2, got) = rest[: len(ops)], rest[len(ops) :]

    @pl.when(level_of(rows_n) > first + 2)
    def _():
        subtract(cols_n, ops, arrived, got, s1, a1, b1, s2)


def pick(cols_n, ops, kind, arrived, got):
    me = place(cols_n)
    any_hit = me < 0
    for op, ref in zip(ops, arrived):
        hit = one_of(me, [t[0] * cols_n + t[1] for _, t, k, _ in op if k == kind])
        any_hit = any_hit | hit

        @pl.when(hit)
        def _():
            got[...] = ref[...]

    return any_hit


def downs(cols_n, first, rows_n, ops, s2, a2, *rest):
    arrived, (s3, got) = rest[: len(ops)], rest[len(ops) :]

    @pl.when(level_of(rows_n) > first + 2)
    def _():
        subtract(cols_n, ops, arrived, got, s2, a2, None, s3, ("down",))


def publish(rows_n, first, f0, f1, f2, out, zeros, sem):
    level = level_of(rows_n)
    for t, block in enumerate((f0, f1, f2)):

        @pl.when(level == first + t)
        def _():
            pltpu.make_async_copy(block, out, sem).start()

    @pl.when((level < first) | (level > first + 2))
    def _():
        zeros[...] = jnp.zeros(zeros.shape, zeros.dtype)
        pltpu.make_async_copy(zeros, out, sem).start()

    pltpu.make_async_copy(zeros, out, sem).wait()


def finish(rows_n, cols_n, first, ops, s3, b2, *rest):
    arrived, (nxt, got, mine, sem) = rest[: len(ops)], rest[len(ops) :]
    n = s3.shape[0]
    step = n // 3
    active = level_of(rows_n) > first + 2

    @pl.when(jnp.logical_not(active))
    def _():
        mine[...] = jnp.zeros(mine.shape, mine.dtype)
        for k in range(3):
            pltpu.make_async_copy(mine.at[pl.ds(k * step, step)], nxt.at[pl.ds(k * step, step)], sem.at[k]).start()

    @pl.when(active)
    def _():
        pick(cols_n, ops, "left", arrived, got)
        for k in range(3):
            rows = pl.ds(k * step, step)
            mine[rows] = s3[rows] - dot(got[rows], b2[...])
            pltpu.make_async_copy(mine.at[rows], nxt.at[rows], sem.at[k]).start()

    for k in range(3):
        pltpu.make_async_copy(mine.at[pl.ds(k * step, step)], nxt.at[pl.ds(k * step, step)], sem.at[k]).wait()


def relay(cols_n, choices, own, *rest):
    *arrived, out = rest
    me = place(cols_n)
    hit = me < 0
    for ids, ref in zip(choices, arrived):
        mine = one_of(me, ids)
        hit = hit | mine

        @pl.when(mine)
        def _():
            out[...] = ref[...]

    @pl.when(jnp.logical_not(hit))
    def _():
        out[...] = own[...]


def spread(ops, cols_n, own, name, call):
    arrived = []
    for k, op in enumerate(ops):
        value = own
        earlier = sorted({f for *_, f in op if f is not None})
        if earlier:
            choices = [[s[0] * cols_n + s[1] for s, _, _, f in op if f == e] for e in earlier]
            (value,) = call(
                functools.partial(relay, cols_n, choices),
                [],
                [own, *[arrived[e] for e in earlier]],
                [jax.ShapeDtypeStruct(own.shape, own.dtype)],
                [],
                f"relay_{name}{k}",
            )
        pairs = [(s[0] * cols_n + s[1], t[0] * cols_n + t[1]) for s, t, _, _ in op]
        arrived.append(move(value, pairs))
    return arrived


def move(value, pairs):
    return lax.ppermute(value, AXES, pairs)


def solution(mesh):
    rows_n, cols_n = mesh.shape["row"], mesh.shape["col"]
    first = (rows_n + cols_n) // 2 - 2
    offset = first - rows_n + 1
    ops0 = chain(rows_n, cols_n, offset)
    ops1 = plan(rows_n, cols_n, offset + 1, 2, 2)
    ops2 = plan(rows_n, cols_n, offset + 2, 1, 1, True)

    def owners(t):
        return [(i, i + offset + t) for i in range(rows_n) if 0 <= i + offset + t < cols_n]

    beside = [
        ((i, j + 2), (i, j + 3), "left", None) for i, j in owners(0) if (j + 2) % 2 == 0 and j + 3 < cols_n
    ]

    def up(t, far):
        return [(i * cols_n + j, (i - far) * cols_n + j) for i, j in owners(t) if i >= far]

    def right(t, far):
        return [(i * cols_n + j, i * cols_n + j + far) for i, j in owners(t) if j + far < cols_n]

    def shards(rhs, a_c, b_c, u, v, a_vals, b_vals):
        n = rhs.shape[0]
        half, full = jnp.bfloat16, jnp.float32
        square = jax.ShapeDtypeStruct((n, n), half)
        wide, tall = jax.ShapeDtypeStruct((n, 3 * n), half), jax.ShapeDtypeStruct((3 * n, n), half)
        state = jax.ShapeDtypeStruct((n, n), full)
        loads = [pltpu.VMEM((n, n), full)] * 3 + [pltpu.VMEM((n,), full)] * 2
        basis_work = [pltpu.VMEM((n, 3 * n), half)] * 2 + [pltpu.VMEM((3 * n, n), half), pltpu.VMEM((n, 3 * n), half), pltpu.VMEM((n, n), full)]
        work = [pltpu.VMEM((n, 3 * n), half), pltpu.VMEM((3 * n, n), half)]

        def call(kernel, far, near, outs, scratch, name):
            ins = [pltpu.with_memory_space_constraint(x, pltpu.HBM) for x in far] + list(near)
            return pl.pallas_call(
                kernel,
                out_shape=outs,
                in_specs=[FAR_SPEC] * len(far) + [VMEM_SPEC] * len(near),
                out_specs=[FAR_SPEC if name in ("finish", "publish") else VMEM_SPEC] * len(outs),
                scratch_shapes=scratch,
                compiler_params=pltpu.CompilerParams(vmem_limit_bytes=24 << 20),
            )(*ins)

        basis_shapes = [wide, wide, tall, wide, state]
        (f0,) = call(
            functools.partial(begin, rows_n, first),
            [rhs, u, v, a_vals, b_vals],
            [],
            [square],
            loads + basis_work + work + [pltpu.SemaphoreType.DMA((5,))],
            "begin",
        )

        def advance(t, down, left, state_in, coup_a, coup_b):
            _, utk, vk, _, _ = basis
            (y,) = call(
                functools.partial(take_left, rows_n, first, t),
                [],
                [left, state_in, coup_b, utk, vk],
                [state],
                work,
                f"left{t}",
            )
            return call(
                functools.partial(finish_solve, rows_n, first, t),
                [],
                [down, y, coup, coup_a, *basis],
                [square],
                work + [pltpu.VMEM((n, n), full)],
                f"solve{t}",
            )

        down = move(f0, up(0, 1))
        left = move(f0, right(0, 1))
        down_far = move(f0, up(0, 2))
        left_far = move(f0, right(0, 2))
        far0 = spread(ops0, cols_n, f0, "a", call)
        far0.append(move(left_far, [(a[0] * cols_n + a[1], b[0] * cols_n + b[1]) for a, b, _, _ in beside]))
        *basis, coup, s, a0, b0, a1, b1, a2, b2 = call(
            functools.partial(prepare, rows_n, first),
            [rhs, a_c, b_c, u, v, a_vals, b_vals],
            [],
            basis_shapes + [wide, state] + [square] * 6,
            loads[1:] + [pltpu.VMEM((2 * n, n), half), pltpu.SemaphoreType.DMA((9,))],
            "prepare",
        )
        (f1,) = advance(0, down, left, s, a0, b0)
        down = move(f1, up(1, 1))
        left = move(f1, right(1, 1))
        (s1,) = call(
            functools.partial(third_early, rows_n, first),
            [],
            [down_far, left_far, s, a0, b0],
            [state],
            [],
            "third_early",
        )
        far1 = spread(ops1, cols_n, f1, "b", call)
        (f2,) = advance(1, down, left, s1, a1, b1)
        for k, (ops, far, a, b) in enumerate(((ops0 + [beside], far0, a0, b0), (ops1, far1, a1, b1))):
            (s,) = call(
                functools.partial(middle, rows_n, cols_n, first, ops),
                [],
                [s, a, b, *far],
                [state],
                [pltpu.VMEM((n, n), half)],
                f"middle{k}",
            )
        lasts = spread(ops2, cols_n, f2, "c", call)
        sent = [k for k, op in enumerate(ops2) if any(kind == "down" for _, _, kind, _ in op)]
        (s3,) = call(
            functools.partial(downs, cols_n, first, rows_n, [ops2[k] for k in sent]),
            [],
            [s, a2, *[lasts[k] for k in sent]],
            [state],
            [pltpu.VMEM((n, n), half)],
            "downs",
        )
        (out,) = call(
            functools.partial(publish, rows_n, first),
            [],
            [f0, f1, f2],
            [square],
            [pltpu.VMEM((n, n), half), pltpu.SemaphoreType.DMA],
            "publish",
        )
        (nxt,) = call(
            functools.partial(finish, rows_n, cols_n, first, ops2),
            [],
            [s3, b2, *lasts],
            [state],
            [pltpu.VMEM((n, n), half), pltpu.VMEM((n, n), full), pltpu.SemaphoreType.DMA((3,))],
            "finish",
        )
        return out, nxt

    placed = (
        P("row", "col"),
        P(None, "row", "col"),
        P(None, "row", "col"),
        P("row", None),
        P("col", None),
        P("row"),
        P("col"),
    )
    return jax.shard_map(
        shards,
        mesh=mesh,
        in_specs=placed,
        out_specs=(P("row", "col"), P("row", "col")),
        check_vma=False,
    )
```

```python
import functools

import jax
import jax.numpy as jnp
from jax import lax
from jax.experimental import pallas as pl
from jax.experimental.pallas import tpu as pltpu
from jax.sharding import PartitionSpec as P


AXES = ("row", "col")
VMEM_SPEC = pl.BlockSpec(memory_space=pltpu.VMEM)
FAR_SPEC = pl.BlockSpec(memory_space=pltpu.HBM)


def plan(rows_n, cols_n, offset, gap, up_gap, apart=False, served=None):
    rights, ups, last = [], [], []
    for i in range(rows_n):
        m = i + offset
        if 0 <= m < cols_n:
            targets = [j for j in range(m + gap, cols_n) if served is None or j // 2 != (m + served) // 2]
            for chip in sorted({j // 2 for j in targets}, reverse=True):
                some = [(i, j) for j in targets if j // 2 == chip]
                (last if chip == m // 2 else rights).append(((i, m), some, "left"))
            above = list(range(i - up_gap + 1))
            ups += [((i, m), [(k, m)], "down") for k in above[:1] + above[1:][-1:] + above[1:-1]]
    todo = rights + ups + last
    ops, forwards = [], []
    while todo:
        used_from, used_to, op = set(), set(), []
        allowed = {"left", "down"}
        if apart:
            turn = {kind for _, _, kind in todo}
            allowed = turn if len(turn) == 1 else {"down" if 0 < len(ops) < 4 else "left"}
        busy = [source for source, _, _ in todo]
        waiting = {targets[0]: busy.count(source) for source, targets, kind in todo if kind == "down"}
        for item in list(todo):
            source, targets, kind = item
            if kind not in allowed or (apart and not ops and item in last and rights):
                continue
            for target in sorted(targets, key=lambda t: (waiting.get(t, 0), -t[1])):
                if source not in used_from and target not in used_to:
                    used_from.add(source)
                    used_to.add(target)
                    op.append((source, target, kind, None))
                    todo.remove(item)
                    forwards += [(target, other, kind, len(ops)) for other in targets if other != target]
                    break
        ops.append(op)
    return ops + [forwards] if forwards else ops


def one_of(me, ids):
    hit = me < 0
    for each in sorted(ids):
        hit = hit | (me == each)
    return hit


def place(cols_n):
    return lax.axis_index("row") * cols_n + lax.axis_index("col")


def level_of(rows_n):
    return rows_n - 1 - lax.axis_index("row") + lax.axis_index("col")


def dot(a, b):
    return lax.dot_general(a, b, (((1,), (0,)), ((), ())), preferred_element_type=jnp.float32)


def split(x):
    high = x.astype(jnp.bfloat16)
    return high, (x - high.astype(jnp.float32)).astype(jnp.bfloat16)


def put_left(ref, pair):
    n = pair[0].shape[1]
    ref[:, 0:n] = pair[0]
    ref[:, n : 2 * n] = pair[0]
    ref[:, 2 * n : 3 * n] = pair[1]


def put_right(ref, pair):
    n = pair[0].shape[0]
    ref[0:n] = pair[0]
    ref[n : 2 * n] = pair[1]
    ref[2 * n : 3 * n] = pair[0]


def dot_t(a, b):
    return lax.dot_general(a, b, (((1,), (1,)), ((), ())), preferred_element_type=jnp.float32)


def spectral(state, utk, vk, lhs, mid):
    put_left(lhs, split(state))
    part = dot(lhs[...], vk[...])
    put_right(mid, split(part))
    return dot(utk[...], mid[...])


def back(part, uk, vl, lhs, mid):
    put_left(lhs, split(part))
    part = dot_t(lhs[...], vl[...])
    put_right(mid, split(part))
    return dot(uk[...], mid[...]).astype(jnp.bfloat16)


def put_lanes(ref, pair):
    n = pair[0].shape[1]
    ref[:, 0:n] = pair[0]
    ref[:, n : 2 * n] = pair[1]
    ref[:, 2 * n : 3 * n] = pair[0]


def set_inverse(inverse, av, bv):
    n = inverse.shape[0]
    alpha = jnp.transpose(jnp.broadcast_to(av[...][None, :], (128, n)))
    beta = bv[...][None, :]
    for c in range(0, n, 128):
        inverse[:, c : c + 128] = 1.0 / (alpha + beta[:, c : c + 128])


def set_right_basis(v, vk, vl):
    pair = split(v[...])
    put_right(vk, pair)
    put_lanes(vl, pair)


def set_left_basis(u, uk, utk):
    high, low = split(u[...])
    put_left(uk, (high, low))
    put_left(utk, (high.T, low.T))


def copies(pairs, sem):
    moves = [pltpu.make_async_copy(source, target, sem.at[n]) for n, (source, target) in enumerate(pairs)]
    for move in moves:
        move.start()
    return moves


def begin(rows_n, first, rhs, u_far, v_far, a_vals, b_vals, f0, s, u, v, av, bv, uk, utk, vk, vl, inverse, lhs, mid, sem):
    @pl.when(level_of(rows_n) == first)
    def _():
        moves = copies(((v_far, v), (rhs, s), (u_far, u), (a_vals, av), (b_vals, bv)), sem)
        moves[0].wait()
        set_right_basis(v, vk, vl)
        for move in moves[1:]:
            move.wait()
        set_left_basis(u, uk, utk)
        set_inverse(inverse, av, bv)
        part = spectral(s[...], utk, vk, lhs, mid) * inverse[...]
        f0[...] = back(part, uk, vl, lhs, mid)


def prepare(rows_n, first, rhs, a_c, b_c, u_far, v_far, a_vals, b_vals, uk, utk, vk, vl, inverse, coup, s, a0, b0, a1, b1, a2, b2, u, v, av, bv, both, sem):
    level = level_of(rows_n)
    terms = ((rhs, s), (a_c.at[0], a0), (b_c.at[0], b0), (a_c.at[1], a1), (b_c.at[1], b1))

    @pl.when((level > first) & (level <= first + 2))
    def _():
        moves = copies(((v_far, v), (u_far, u), (a_vals, av), (b_vals, bv), *terms), sem)
        moves[0].wait()
        set_right_basis(v, vk, vl)
        moves[1].wait()
        set_left_basis(u, uk, utk)
        moves[2].wait()
        moves[3].wait()
        set_inverse(inverse, av, bv)
        for move in moves[4:]:
            move.wait()
        n = u.shape[0]
        for t, a in enumerate((a0, a1)):

            @pl.when(level == first + 1 + t)
            def _():
                both[0:n] = a[...]
                both[n:] = a[...]

        put_left(coup, split(dot(utk[:, n:], both[...])))

    @pl.when(level > first + 2)
    def _():
        for move in copies((*terms, (a_c.at[2], a2), (b_c.at[2], b2)), sem):
            move.wait()


def late(t):
    return (lax.rem(lax.axis_index("col"), 2) == 0) & (t == 1)


def take_left(rows_n, first, t, left, s, coup_b, utk, vk, out, lhs, mid):
    mine = level_of(rows_n) == first + t + 1

    @pl.when(mine)
    def _():
        out[...] = s[...] - dot(left[...], coup_b[...])

    @pl.when(mine & jnp.logical_not(late(t)))
    def _():
        out[...] = spectral(out[...], utk, vk, lhs, mid)


def finish_solve(rows_n, first, t, down, y, coup, coup_a, uk, utk, vk, vl, inverse, f, lhs, mid, part):
    mine = level_of(rows_n) == first + t + 1

    @pl.when(mine & late(t))
    def _():
        part[...] = spectral(y[...] - dot(coup_a[...], down[...]), utk, vk, lhs, mid) * inverse[...]

    @pl.when(mine & jnp.logical_not(late(t)))
    def _():
        n = y.shape[0]
        lhs[:, 0:n] = down[...]
        lhs[:, n : 2 * n] = down[...]
        put_right(mid, split(dot(lhs[:, 0 : 2 * n], vk[0 : 2 * n])))
        part[...] = (y[...] - dot(coup[...], mid[...])) * inverse[...]

    @pl.when(mine)
    def _():
        f[...] = back(part[...], uk, vl, lhs, mid)


def third_early(rows_n, first, down, left, s, a0, b0, s1):
    @pl.when(level_of(rows_n) == first + 2)
    def _():
        s1[...] = s[...] - (dot(a0[...], down[...]) + dot(left[...], b0[...]))


def subtract(cols_n, ops, arrived, got, state, coup_a, coup_b, out, kinds=("down", "left")):
    out[...] = state[...]
    for kind in kinds:
        hits = pick(cols_n, ops, kind, arrived, got)

        @pl.when(hits)
        def _():
            out[...] -= dot(got[...], coup_b[...]) if kind == "left" else dot(coup_a[...], got[...])


def middle(rows_n, cols_n, first, ops, s1, a1, b1, *rest):
    arrived, (s2, got) = rest[: len(ops)], rest[len(ops) :]

    @pl.when(level_of(rows_n) > first + 2)
    def _():
        subtract(cols_n, ops, arrived, got, s1, a1, b1, s2)


def pick(cols_n, ops, kind, arrived, got):
    me = place(cols_n)
    any_hit = me < 0
    for op, ref in zip(ops, arrived):
        hit = one_of(me, [t[0] * cols_n + t[1] for _, t, k, _ in op if k == kind])
        any_hit = any_hit | hit

        @pl.when(hit)
        def _():
            got[...] = ref[...]

    return any_hit


def downs(cols_n, first, rows_n, ops, s2, a2, *rest):
    arrived, (s3, got) = rest[: len(ops)], rest[len(ops) :]

    @pl.when(level_of(rows_n) > first + 2)
    def _():
        subtract(cols_n, ops, arrived, got, s2, a2, None, s3, ("down",))


def publish(rows_n, first, f0, f1, f2, out, zeros, sem):
    level = level_of(rows_n)
    for t, block in enumerate((f0, f1, f2)):

        @pl.when(level == first + t)
        def _():
            pltpu.make_async_copy(block, out, sem).start()

    @pl.when((level < first) | (level > first + 2))
    def _():
        zeros[...] = jnp.zeros(zeros.shape, zeros.dtype)
        pltpu.make_async_copy(zeros, out, sem).start()

    pltpu.make_async_copy(zeros, out, sem).wait()


def finish(rows_n, cols_n, first, ops, s3, b2, *rest):
    arrived, (nxt, got, mine, sem) = rest[: len(ops)], rest[len(ops) :]
    n = s3.shape[0]
    step = n // 3
    active = level_of(rows_n) > first + 2

    @pl.when(jnp.logical_not(active))
    def _():
        mine[...] = jnp.zeros(mine.shape, mine.dtype)
        for k in range(3):
            pltpu.make_async_copy(mine.at[pl.ds(k * step, step)], nxt.at[pl.ds(k * step, step)], sem.at[k]).start()

    @pl.when(active)
    def _():
        pick(cols_n, ops, "left", arrived, got)
        for k in range(3):
            rows = pl.ds(k * step, step)
            mine[rows] = s3[rows] - dot(got[rows], b2[...])
            pltpu.make_async_copy(mine.at[rows], nxt.at[rows], sem.at[k]).start()

    for k in range(3):
        pltpu.make_async_copy(mine.at[pl.ds(k * step, step)], nxt.at[pl.ds(k * step, step)], sem.at[k]).wait()


def relay(cols_n, choices, own, *rest):
    *arrived, out = rest
    me = place(cols_n)
    hit = me < 0
    for ids, ref in zip(choices, arrived):
        mine = one_of(me, ids)
        hit = hit | mine

        @pl.when(mine)
        def _():
            out[...] = ref[...]

    @pl.when(jnp.logical_not(hit))
    def _():
        out[...] = own[...]


def spread(ops, cols_n, own, name, call):
    arrived = []
    for k, op in enumerate(ops):
        value = own
        earlier = sorted({f for *_, f in op if f is not None})
        if earlier:
            choices = [[s[0] * cols_n + s[1] for s, _, _, f in op if f == e] for e in earlier]
            (value,) = call(
                functools.partial(relay, cols_n, choices),
                [],
                [own, *[arrived[e] for e in earlier]],
                [jax.ShapeDtypeStruct(own.shape, own.dtype)],
                [],
                f"relay_{name}{k}",
            )
        pairs = [(s[0] * cols_n + s[1], t[0] * cols_n + t[1]) for s, t, _, _ in op]
        arrived.append(move(value, pairs))
    return arrived


def move(value, pairs):
    return lax.ppermute(value, AXES, pairs)


def solution(mesh):
    rows_n, cols_n = mesh.shape["row"], mesh.shape["col"]
    first = (rows_n + cols_n) // 2 - 2
    offset = first - rows_n + 1
    ops0 = plan(rows_n, cols_n, offset, 3, 3, served=2)
    ops1 = plan(rows_n, cols_n, offset + 1, 2, 2)
    ops2 = plan(rows_n, cols_n, offset + 2, 1, 1, True)

    def owners(t):
        return [(i, i + offset + t) for i in range(rows_n) if 0 <= i + offset + t < cols_n]

    beside = [
        ((i, j + 2), (i, j + 3), "left", None) for i, j in owners(0) if (j + 2) % 2 == 0 and j + 3 < cols_n
    ]

    def up(t, far):
        return [(i * cols_n + j, (i - far) * cols_n + j) for i, j in owners(t) if i >= far]

    def right(t, far):
        return [(i * cols_n + j, i * cols_n + j + far) for i, j in owners(t) if j + far < cols_n]

    def shards(rhs, a_c, b_c, u, v, a_vals, b_vals):
        n = rhs.shape[0]
        half, full = jnp.bfloat16, jnp.float32
        square = jax.ShapeDtypeStruct((n, n), half)
        wide, tall = jax.ShapeDtypeStruct((n, 3 * n), half), jax.ShapeDtypeStruct((3 * n, n), half)
        state = jax.ShapeDtypeStruct((n, n), full)
        loads = [pltpu.VMEM((n, n), full)] * 3 + [pltpu.VMEM((n,), full)] * 2
        basis_work = [pltpu.VMEM((n, 3 * n), half)] * 2 + [pltpu.VMEM((3 * n, n), half), pltpu.VMEM((n, 3 * n), half), pltpu.VMEM((n, n), full)]
        work = [pltpu.VMEM((n, 3 * n), half), pltpu.VMEM((3 * n, n), half)]

        def call(kernel, far, near, outs, scratch, name):
            ins = [pltpu.with_memory_space_constraint(x, pltpu.HBM) for x in far] + list(near)
            return pl.pallas_call(
                kernel,
                out_shape=outs,
                in_specs=[FAR_SPEC] * len(far) + [VMEM_SPEC] * len(near),
                out_specs=[FAR_SPEC if name in ("finish", "publish") else VMEM_SPEC] * len(outs),
                scratch_shapes=scratch,
                compiler_params=pltpu.CompilerParams(vmem_limit_bytes=24 << 20),
            )(*ins)

        basis_shapes = [wide, wide, tall, wide, state]
        (f0,) = call(
            functools.partial(begin, rows_n, first),
            [rhs, u, v, a_vals, b_vals],
            [],
            [square],
            loads + basis_work + work + [pltpu.SemaphoreType.DMA((5,))],
            "begin",
        )

        def advance(t, down, left, state_in, coup_a, coup_b):
            _, utk, vk, _, _ = basis
            (y,) = call(
                functools.partial(take_left, rows_n, first, t),
                [],
                [left, state_in, coup_b, utk, vk],
                [state],
                work,
                f"left{t}",
            )
            return call(
                functools.partial(finish_solve, rows_n, first, t),
                [],
                [down, y, coup, coup_a, *basis],
                [square],
                work + [pltpu.VMEM((n, n), full)],
                f"solve{t}",
            )

        down = move(f0, up(0, 1))
        left = move(f0, right(0, 1))
        down_far = move(f0, up(0, 2))
        left_far = move(f0, right(0, 2))
        far0 = spread(ops0, cols_n, f0, "a", call)
        far0.append(move(left_far, [(a[0] * cols_n + a[1], b[0] * cols_n + b[1]) for a, b, _, _ in beside]))
        *basis, coup, s, a0, b0, a1, b1, a2, b2 = call(
            functools.partial(prepare, rows_n, first),
            [rhs, a_c, b_c, u, v, a_vals, b_vals],
            [],
            basis_shapes + [wide, state] + [square] * 6,
            loads[1:] + [pltpu.VMEM((2 * n, n), half), pltpu.SemaphoreType.DMA((9,))],
            "prepare",
        )
        (f1,) = advance(0, down, left, s, a0, b0)
        down = move(f1, up(1, 1))
        left = move(f1, right(1, 1))
        (s1,) = call(
            functools.partial(third_early, rows_n, first),
            [],
            [down_far, left_far, s, a0, b0],
            [state],
            [],
            "third_early",
        )
        far1 = spread(ops1, cols_n, f1, "b", call)
        (f2,) = advance(1, down, left, s1, a1, b1)
        for k, (ops, far, a, b) in enumerate(((ops0 + [beside], far0, a0, b0), (ops1, far1, a1, b1))):
            (s,) = call(
                functools.partial(middle, rows_n, cols_n, first, ops),
                [],
                [s, a, b, *far],
                [state],
                [pltpu.VMEM((n, n), half)],
                f"middle{k}",
            )
        lasts = spread(ops2, cols_n, f2, "c", call)
        sent = [k for k, op in enumerate(ops2) if any(kind == "down" for _, _, kind, _ in op)]
        (s3,) = call(
            functools.partial(downs, cols_n, first, rows_n, [ops2[k] for k in sent]),
            [],
            [s, a2, *[lasts[k] for k in sent]],
            [state],
            [pltpu.VMEM((n, n), half)],
            "downs",
        )
        (out,) = call(
            functools.partial(publish, rows_n, first),
            [],
            [f0, f1, f2],
            [square],
            [pltpu.VMEM((n, n), half), pltpu.SemaphoreType.DMA],
            "publish",
        )
        (nxt,) = call(
            functools.partial(finish, rows_n, cols_n, first, ops2),
            [],
            [s3, b2, *lasts],
            [state],
            [pltpu.VMEM((n, n), half), pltpu.VMEM((n, n), full), pltpu.SemaphoreType.DMA((3,))],
            "finish",
        )
        return out, nxt

    placed = (
        P("row", "col"),
        P(None, "row", "col"),
        P(None, "row", "col"),
        P("row", None),
        P("col", None),
        P("row"),
        P("col"),
    )
    return jax.shard_map(
        shards,
        mesh=mesh,
        in_specs=placed,
        out_specs=(P("row", "col"), P("row", "col")),
        check_vma=False,
    )
```
